256 devices in a mesh: tm: 8 (over y, core), strip: 32 (over z, x).
Axes of the slice: x: 4, y: 4, z: 8, core: 2. Of those that a mesh axis runs over, the one named last changes fastest.
Arguments:
- start_state: float32 [16, 256, 128], P(None, 'strip'), may hold values from -20 to 20
- trajectory: float32 [16, 16, 256, 128], P('tm', None, 'strip'), may hold values from -20 to 20
- history: float32 [3, 16, 16, 256, 128], P(None, 'tm', None, 'strip'), may hold values from -6 to 6
- history_length: int32 [16], P('tm'), may hold values from 1 to 3
- timesteps: int32 [16], P('tm'), may hold values from 0 to 999
- step_size: float32 [16], P('tm'), may hold values from 0.05 to 0.2
- mix_table: int32 [16, 16], replicated, may hold values from -64 to 128, as said below
- time_table: float32 [1000, 320], replicated, may hold values from -6 to 6
- conv_in: bfloat16 [9, 320, 16], replicated, may hold values from -0.5 to 0.5
- norm_gain: float32 [320], replicated, may hold values from 0.1 to 1.9
- norm_bias: float32 [320], replicated, may hold values from -3 to 3
- conv_mid: bfloat16 [9, 320, 320], replicated, may hold values from -0.109375 to 0.109375
- conv_out: bfloat16 [16, 320], replicated, may hold values from -0.3125 to 0.3125
Outputs:
- iterate: float32 [16, 16, 256, 128], P('tm', None, 'strip')
- residual: float32 [16, 16, 256, 128], P('tm', None, 'strip')
The draws below stay inside these ranges and needn't reach their ends.
Inputs may be any that keep to these rules, and one draw needn't show every extreme that they name: mix_table[j, i] is 0 for i > j and lies in 64 to 128 for i = j.
All inputs are finite; a program needn't handle non-finite values.
Results may differ from the reference program's by a relative error of at most 0.001.
Values may be sent and summed in bfloat16 or wider, within the bound.
A program may use at most 128 MiB of HBM per device.

```python
import math
import jax
import jax.numpy as jnp
from jax import lax

CIN = 16
CH = 320
GROUPS = 32
NTIME = 1000
HIST = 3
ITERS = 2
WIDTH = 128
STEPS = 16
HEIGHT = 256


def draw_start_state(key, part):
    shape = (CIN, HEIGHT, WIDTH)
    rows = jnp.arange(HEIGHT, dtype=jnp.float32) / max(HEIGHT - 1, 1)
    base = jnp.clip(jax.random.normal(key, shape, jnp.float32), -6.0, 6.0)
    return base * (3.0 ** rows)[:, None]


def draw_trajectory(key, part):
    shape = (STEPS, CIN, HEIGHT, WIDTH)
    rows = jnp.arange(HEIGHT, dtype=jnp.float32) / max(HEIGHT - 1, 1)
    base = jnp.clip(jax.random.normal(key, shape, jnp.float32), -4.0, 4.0)
    return base * (3.0 ** rows)[:, None] + (1.0 + 3.0 * rows)[:, None]


def draw_mix_table(key, part):
    first_key, second_key = jax.random.split(jax.random.fold_in(key, 11))
    below = jax.random.randint(first_key, (STEPS, STEPS), -64, 65, dtype=jnp.int32)
    middle = jax.random.randint(second_key, (STEPS,), 64, 129, dtype=jnp.int32)
    row_index = jnp.arange(STEPS, dtype=jnp.int32)[:, None]
    col_index = jnp.arange(STEPS, dtype=jnp.int32)[None, :]
    middle_full = jnp.broadcast_to(middle[:, None], (STEPS, STEPS))
    return jnp.where(col_index < row_index, below, jnp.where(col_index == row_index, middle_full, jnp.zeros_like(below)))


def plant(drawn, own_key, low, high):
    longest = drawn.shape.index(max(drawn.shape))
    spots = []
    for shift in (0, 1):
        where = [jax.random.randint(jax.random.fold_in(own_key, axis), (), 0, length) for axis, length in enumerate(drawn.shape)]
        where[longest] = (where[longest] + shift) % drawn.shape[longest]
        spots.append(tuple(where))
    return drawn.at[spots[0]].set(low).at[spots[1]].set(high)


def steps_of(stream_key, dims, pieces, smallest, high):
    level, own = 1.0, jax.random.fold_in(stream_key, 6)
    for dim, shards_of in pieces:
        steps = jnp.exp(jax.random.uniform(jax.random.fold_in(own, dim), (shards_of,), jnp.float32, smallest / len(pieces), high / len(pieces)))
        level = level * jnp.repeat(steps, dims[dim] // shards_of).reshape([-1 if axis == dim else 1 for axis in range(len(dims))])
    return level


def gaussian(own_key, shape, deviation, bound, cuts=(), kind=jnp.bfloat16):
    level = steps_of(own_key, shape, cuts, -0.22, 0.18) if cuts else 1.0
    drawn = jax.random.normal(own_key, shape, jnp.float32) * deviation * level
    return jnp.minimum(jnp.maximum(drawn, -bound), bound).astype(kind)


def setup_inputs(seed: int = 0) -> dict:
    key_list = jax.random.split(jax.random.key(seed), 14)
    return {
        "start_state": draw_start_state(jax.random.fold_in(key_list[13], 71), 0),
        "trajectory": draw_trajectory(jax.random.fold_in(key_list[13], 71), 0),
        "history": gaussian(key_list[2], (HIST, STEPS, CIN, HEIGHT, WIDTH), 1.0, 6.0, ((1, 8), (3, 32)), jnp.float32),
        "history_length": plant(jax.random.randint(key_list[3], (STEPS,), 1, HIST + 1), jax.random.fold_in(key_list[3], 1), 1, HIST).astype(jnp.int32),
        "timesteps": plant(jax.random.randint(key_list[4], (STEPS,), 0, NTIME), jax.random.fold_in(key_list[4], 1), 0, NTIME - 1).astype(jnp.int32),
        "step_size": jnp.clip(jnp.exp(math.log(0.2) - 1.3862944 * jax.random.uniform(key_list[5], (STEPS,), jnp.float32) ** steps_of(key_list[5], (STEPS,), ((0, 8),), -0.2, 0.2)), 0.05, 0.2),
        "mix_table": draw_mix_table(jax.random.fold_in(key_list[13], 71), 0),
        "time_table": gaussian(key_list[7], (NTIME, CH), 1.0, 6.0, (), jnp.float32),
        "conv_in": gaussian(key_list[8], (9, CH, CIN), (9 * CIN) ** -0.5, 0.5),
        "norm_gain": jnp.clip(1.0 + 0.18 * jax.random.normal(key_list[9], (CH,), jnp.float32), 0.1, 1.9),
        "norm_bias": gaussian(key_list[10], (CH,), 0.5, 3.0, (), jnp.float32),
        "conv_mid": gaussian(key_list[11], (9, CH, CH), (9 * CH) ** -0.5, 0.109375),
        "conv_out": gaussian(key_list[12], (CIN, CH), CH ** -0.5, 0.3125),
    }


epsilon = 1e-05
coefficient_unit = 256.0

def convolve(padded_rows, weights):
    height = padded_rows.shape[-2] - 2
    width = padded_rows.shape[-1]
    padded = jnp.pad(padded_rows, ((0, 0), (0, 0), (1, 1))).astype(jnp.float32)
    total = jnp.zeros((weights.shape[1], height, width), jnp.float32)
    for row_tap in range(3):
        for col_tap in range(3):
            window = padded[:, row_tap:row_tap + height, col_tap:col_tap + width]
            total = total + jnp.einsum('oc,chw->ohw', weights[3 * row_tap + col_tap].astype(jnp.float32), window, precision=lax.Precision.HIGHEST)
    return total

def denoise(state_bf, embed_row, conv_in, norm_gain, norm_bias, conv_mid, conv_out):
    early = convolve(jnp.pad(state_bf, ((0, 0), (1, 1), (0, 0))), conv_in) + embed_row[:, None, None]
    channels, height, width = early.shape
    grouped = early.reshape(GROUPS, channels // GROUPS, height, width)
    mean = lax.optimization_barrier(jnp.mean(grouped, axis=(1, 2, 3), keepdims=True))
    variance = lax.optimization_barrier(jnp.mean((grouped - mean) * (grouped - mean), axis=(1, 2, 3), keepdims=True))
    normed = ((grouped - mean) / jnp.sqrt(variance + epsilon)).reshape(channels, height, width)
    hidden = jax.nn.silu(normed * norm_gain[:, None, None] + norm_bias[:, None, None]).astype(jnp.bfloat16)
    late = convolve(jnp.pad(hidden, ((0, 0), (1, 1), (0, 0))), conv_mid)
    active = jax.nn.silu(late).astype(jnp.bfloat16)
    return jnp.einsum('oc,chw->ohw', conv_out.astype(jnp.float32), active.astype(jnp.float32), precision=lax.Precision.HIGHEST)

def reference(start_state, trajectory, history, history_length, timesteps, step_size, mix_table, time_table, conv_in, norm_gain, norm_bias, conv_mid, conv_out):
    selector = (timesteps[:, None] == jnp.arange(time_table.shape[0], dtype=jnp.int32)[None, :]).astype(jnp.float32)
    embedding = jnp.dot(selector, time_table, precision=lax.Precision.HIGHEST)
    coefficient = mix_table.astype(jnp.float32) / coefficient_unit
    levels = jnp.arange(history.shape[0], dtype=jnp.int32)[:, None]
    live = (levels < history_length[None, :]).astype(jnp.float32) / history_length[None, :].astype(jnp.float32)
    state = trajectory
    past = history
    residual = jnp.zeros_like(trajectory)
    for sweep in range(ITERS):
        field = lax.map(lambda pair: denoise(pair[0], pair[1], conv_in, norm_gain, norm_bias, conv_mid, conv_out), (state.astype(jnp.bfloat16), embedding))
        drift = step_size[:, None, None, None] * field
        running = jnp.cumsum(drift, axis=0)
        before = jnp.concatenate([jnp.zeros_like(drift[:1]), running[:-1]], axis=0)
        guess = start_state[None] + before
        residual = guess - state
        anchor = residual - jnp.einsum('ms,mschw->schw', live, past, precision=lax.Precision.HIGHEST)
        correction = jnp.einsum('ji,ichw->jchw', coefficient, anchor, precision=lax.Precision.HIGHEST)
        state = guess + correction
        past = jnp.concatenate([residual[None], past[:-1]], axis=0)
    return (state, residual)
```

```python
import functools

import jax
import jax.numpy as jnp
from jax import lax
from jax.experimental import pallas as pl
from jax.experimental.pallas import tpu as pltpu
from jax.sharding import PartitionSpec as P

F32 = jnp.float32
BF16 = jnp.bfloat16
HIGHEST = lax.Precision.HIGHEST
GROUPS = 32
ITERS = 2
EPSILON = 1e-05
UNIT = 1.0 / 256.0
LANES = 128
CHUNK = 32


def silu(v):
    half = 0.5 * v
    return half + half * jnp.tanh(half)


def kernel(
    T,
    S,
    hl_ref,
    ts_ref,
    step_ref,
    mix_ref,
    gain_ref,
    bias_ref,
    start_ref,
    traj_ref,
    hist_ref,
    cin_ref,
    cout_ref,
    table_hbm,
    cmid_hbm,
    iterate_ref,
    residual_ref,
    table,
    wraw,
    wmid,
    win,
    xin,
    xs,
    early,
    hid,
    gaincol,
    biascol,
    embcol,
    ind,
    sums,
    stat,
    stats,
    fsend,
    frecv,
    msend,
    mrecv,
    sbuf,
    state1,
    base2,
    osend,
    orecv,
    local_sem,
    halo_send,
    halo_recv,
    m_send,
    m_recv,
    s_send,
    s_recv,
    a_send,
    a_recv,
    b_send,
    b_recv,
    o_send,
    o_recv,
):
    t = lax.axis_index("tm")
    s = lax.axis_index("strip")
    steps = 2
    CH = cout_ref.shape[1]
    CIN = cout_ref.shape[0]
    rows = T
    total_steps = steps * T
    count = float(CH // GROUPS * rows * S * LANES)

    def to(src, dst, send, recv, tm, strip):
        return pltpu.make_async_remote_copy(
            src_ref=src,
            dst_ref=dst,
            send_sem=send,
            recv_sem=recv,
            device_id=(tm, strip),
            device_id_type=pl.DeviceIdType.MESH,
        )

    def wait_bytes(ref, sem):
        pltpu.make_async_copy(ref, ref, sem).wait()

    get_table = pltpu.make_async_copy(table_hbm, table, local_sem.at[0])
    get_mid = pltpu.make_async_copy(cmid_hbm, wraw, local_sem.at[1])
    get_table.start()
    get_mid.start()

    for j in range(steps):
        for h in range(rows):
            xin[0, 2 + h, j] = traj_ref[pl.ds(j * CIN * rows + h, CIN, stride=rows), :].astype(BF16)
    send_down = to(xin.at[0, pl.ds(rows, 2)], xin.at[0, pl.ds(0, 2)], halo_send.at[0], halo_recv.at[0], t, s + 1)
    send_up = to(xin.at[0, pl.ds(2, 2)], xin.at[0, pl.ds(rows + 2, 2)], halo_send.at[1], halo_recv.at[1], t, s - 1)

    @pl.when(s < S - 1)
    def _():
        send_down.start()

    @pl.when(s > 0)
    def _():
        send_up.start()

    @pl.when(s == 0)
    def _():
        xin[0, 0:2] = jnp.zeros((2, steps, CIN, LANES), BF16)
        xin[1, 0:2] = jnp.zeros((2, steps, CIN, LANES), BF16)

    @pl.when(s == S - 1)
    def _():
        xin[0, rows + 2 : rows + 4] = jnp.zeros((2, steps, CIN, LANES), BF16)
        xin[1, rows + 2 : rows + 4] = jnp.zeros((2, steps, CIN, LANES), BF16)

    for j in range(steps):
        length = jnp.full((CIN, LANES), hl_ref[j], jnp.int32)
        share = 1.0 / length.astype(F32)
        live = [jnp.where(length > m, share, 0.0) for m in range(3)]
        for h in range(rows):
            own = traj_ref[pl.ds(j * CIN * rows + h, CIN, stride=rows), :]
            past = [
                hist_ref[pl.ds((m * steps + j) * CIN * rows + h, CIN, stride=rows), :] for m in range(3)
            ]
            msend[h, j, 0:CIN] = own + (live[0] * past[0] + live[1] * past[1] + live[2] * past[2])
            msend[h, j, CIN : 2 * CIN] = live[1] * past[0] + live[2] * past[1] - live[0] * own
            msend[h, j, 2 * CIN : 2 * CIN + 8] = live[0][0:8]
    mrecv[t] = msend[t]

    def send_m(k, _):
        other = lax.rem(t + k, T)
        to(msend.at[other], mrecv.at[t], m_send, m_recv, other, s).start()
        return 0

    lax.fori_loop(1, T, send_m, 0)

    row_id = lax.broadcasted_iota(jnp.int32, (CH, CH), 0)
    col_id = lax.broadcasted_iota(jnp.int32, (CH, CH), 1)
    diagonal = row_id == col_id
    gaincol[...] = jnp.sum(
        jnp.where(diagonal, jnp.broadcast_to(gain_ref[...], (CH, CH)), 0.0), axis=1, keepdims=True
    )
    biascol[...] = jnp.sum(
        jnp.where(diagonal, jnp.broadcast_to(bias_ref[...], (CH, CH)), 0.0), axis=1, keepdims=True
    )
    turned = lax.dot_general(
        diagonal.astype(F32).astype(BF16),
        cin_ref[...],
        (((1,), (1,)), ((), ())),
        preferred_element_type=F32,
    )
    win[...] = turned.astype(BF16)
    members = CH // GROUPS
    first = lax.broadcasted_iota(jnp.int32, (2 * CH, LANES), 1) * members
    channel = lax.broadcasted_iota(jnp.int32, (2 * CH, LANES), 0)
    ind[...] = jnp.where((channel >= first) & (channel < first + members), 1.0, 0.0)
    get_table.wait()
    at = lax.broadcasted_iota(jnp.int32, table.shape, 1)
    for j in range(steps):
        embcol[j] = jnp.sum(jnp.where(at == ts_ref[j], table[...], 0.0), axis=1, keepdims=True)

    get_mid.wait()
    low = lax.broadcasted_iota(jnp.int32, (CH, LANES), 1) < 64
    for a in range(3):
        wmid[a, :, 0:256] = wraw[3 * a, :, 0:256]
        wmid[a, :, 640:960] = wraw[3 * a + 2]
        middle = [wraw[3 * a + 1, :, k * LANES : (k + 1) * LANES].astype(F32) for k in range(2)]
        tail = wraw[3 * a + 1, :, 256:320].astype(F32)
        middle.append(jnp.concatenate([tail, tail], axis=1))
        turned_by = [pltpu.roll(m, 64, 1) for m in middle[:2]] + [middle[2]]
        head = wraw[3 * a, :, 256:320].astype(F32)
        before = jnp.concatenate([head, head], axis=1)
        for k in range(3):
            wmid[a, :, 256 + k * LANES : 256 + (k + 1) * LANES] = jnp.where(
                low, before, turned_by[k]
            ).astype(BF16)
            before = turned_by[k]

    @pl.when(s < S - 1)
    def _():
        send_down.wait_send()

    @pl.when(s > 0)
    def _():
        send_up.wait_send()

    @pl.when(s > 0)
    def _():
        send_down.wait_recv()

    @pl.when(s < S - 1)
    def _():
        send_up.wait_recv()

    lane = lax.broadcasted_iota(jnp.int32, (CIN, LANES), 1)
    wide = lax.broadcasted_iota(jnp.int32, (CHUNK, LANES), 1)

    def shifted(x, lanes):
        left = jnp.where(lanes == 0, 0.0, pltpu.roll(x, 1, 1))
        right = jnp.where(lanes == LANES - 1, 0.0, pltpu.roll(x, LANES - 1, 1))
        return left, right

    def first_conv(it, j):
        for r in range(rows + 4):
            block = xin[it, r, j]
            left, right = shifted(block.astype(F32), lane)
            xs[0:CIN, r * LANES : (r + 1) * LANES] = left.astype(BF16)
            xs[CIN : 2 * CIN, r * LANES : (r + 1) * LANES] = block
            xs[2 * CIN : 3 * CIN, r * LANES : (r + 1) * LANES] = right.astype(BF16)
        for r in range(0, rows + 2, 2):
            taps = jnp.concatenate(
                [xs[:, (r + a) * LANES : (r + a + 2) * LANES] for a in range(3)], axis=0
            )
            early[j, :, r * LANES : (r + 2) * LANES] = (
                jnp.dot(win[...], taps, preferred_element_type=F32) + embcol[j]
            )

    def send_sums(it, j):
        k = it * steps + j

        def add_up(c, _):
            at = pl.multiple_of(c * CHUNK, CHUNK)
            total = jnp.zeros((CHUNK, LANES), F32)
            square = jnp.zeros((CHUNK, LANES), F32)
            for r in range(1, rows + 1):
                x = early[j, pl.ds(at, CHUNK), r * LANES : (r + 1) * LANES]
                total += x
                square += x * x
            sums[pl.ds(at, CHUNK)] = total
            sums[pl.ds(CH + at, CHUNK)] = square
            return 0

        lax.fori_loop(0, CH // CHUNK, add_up, 0)
        by_channel = lax.dot_general(
            jnp.ones((8, LANES), F32), sums[...], (((1,), (1,)), ((), ())), precision=HIGHEST,
            preferred_element_type=F32,
        )
        by_group = jnp.dot(by_channel, ind[...], precision=HIGHEST, preferred_element_type=F32)
        stat[k] = by_group[0:1]
        stats[k, s] = by_group[0:1]

        def send(i, _):
            other = lax.rem(s + i, S)
            to(stat.at[k], stats.at[k, s], s_send.at[k], s_recv.at[k], t, other).start()
            return 0

        lax.fori_loop(1, S, send, 0)

    def normalise(it, j):
        k = it * steps + j
        wait_bytes(stats.at[k, pl.ds(0, S - 1)], s_send.at[k])
        wait_bytes(stats.at[k, pl.ds(0, S - 1)], s_recv.at[k])
        total = jnp.sum(stats[k], axis=0) * (1.0 / count)
        total = jnp.broadcast_to(total, (8, LANES))
        variance = jnp.maximum(pltpu.roll(total, LANES - GROUPS, 1) - total * total, 0.0)
        scale = 1.0 / jnp.sqrt(variance + EPSILON)
        mean_row, scale_row = total[0:1], scale[0:1]

        def body(c, _):
            at = pl.multiple_of(c * CHUNK, CHUNK)
            which = ind[pl.ds(at, CHUNK)]
            mean = jnp.sum(jnp.where(which > 0.5, mean_row, 0.0), axis=1, keepdims=True)
            factor = jnp.sum(jnp.where(which > 0.5, scale_row, 0.0), axis=1, keepdims=True)
            factor = factor * gaincol[pl.ds(at, CHUNK)]
            offset = biascol[pl.ds(at, CHUNK)]
            for r in range(rows + 2):
                x = early[j, pl.ds(at, CHUNK), r * LANES : (r + 1) * LANES]
                x = silu((x - mean) * factor + offset)
                if r == 0:
                    x = jnp.where(s > 0, x, 0.0)
                if r == rows + 1:
                    x = jnp.where(s < S - 1, x, 0.0)
                left, right = shifted(x, wide)
                cells = slice(r * LANES, (r + 1) * LANES)
                hid[j, pl.ds(at, CHUNK), cells] = left.astype(BF16)
                hid[j, pl.ds(CH + at, CHUNK), cells] = x.astype(BF16)
                hid[j, pl.ds(2 * CH + at, CHUNK), cells] = right.astype(BF16)
            return 0

        lax.fori_loop(0, CH // CHUNK, body, 0)

    def second_conv(it, j):
        for p in range(rows // 2):
            late = None
            for a in range(3):
                product = jnp.dot(
                    wmid[a],
                    hid[j, :, (2 * p + a) * LANES : (2 * p + a + 2) * LANES],
                    preferred_element_type=F32,
                )
                late = product if late is None else late + product
            active = silu(late).astype(BF16)
            field = jnp.dot(cout_ref[...], active, preferred_element_type=F32)
            drift = field * step_ref[j]
            for h in range(2):
                row = 2 * p + h
                fsend[it, row, j] = drift[:, h * LANES : (h + 1) * LANES]

                @pl.when(t == row)
                def _():
                    frecv[it, row, j] = drift[:, h * LANES : (h + 1) * LANES]

                @pl.when(t != row)
                def _():
                    to(fsend.at[it, row, j], frecv.at[it, t, j], a_send.at[it], a_recv.at[it], row, s).start()

    def row_guess(it):
        wait_bytes(frecv.at[it, pl.ds(0, T - 1)], a_send.at[it])
        wait_bytes(frecv.at[it, pl.ds(0, T - 1)], a_recv.at[it])
        guess = [start_ref[pl.ds(t, CIN, stride=rows), :]]
        for i in range(total_steps - 1):
            guess.append(guess[-1] + frecv[it, i // steps, i % steps])
        return guess

    def mixed(guess, anchor, j):
        total = guess[j]
        for i in range(j + 1):
            total = total + (mix_ref[j, i].astype(F32) * UNIT) * anchor[i]
        return total

    for it in range(ITERS):
        for j in range(steps):
            first_conv(it, j)
            send_sums(it, j)
        for j in range(steps):
            normalise(it, j)
            second_conv(it, j)
        if it == 0:
            wait_bytes(mrecv.at[pl.ds(0, T - 1)], m_send)
            wait_bytes(mrecv.at[pl.ds(0, T - 1)], m_recv)
            guess = row_guess(it)
            anchor = [
                guess[i] - mrecv[i // steps, i % steps, 0:CIN] for i in range(total_steps)
            ]
            for j in range(total_steps):
                new = mixed(guess, anchor, j)
                sbuf[j] = new.astype(BF16)
                state1[j] = new
                share = mrecv[j // steps, j % steps, 2 * CIN : 2 * CIN + 8]
                share = jnp.concatenate([share, share], axis=0)
                base2[j] = new + (share * guess[j] + mrecv[j // steps, j % steps, CIN : 2 * CIN])
            xin[1, 2 + t] = sbuf[pl.ds(steps * t, steps)]

            def send_row(k, _):
                other = lax.rem(t + k, T)
                to(sbuf.at[pl.ds(steps * other, steps)], xin.at[1, 2 + t], b_send.at[0], b_recv.at[0], other, s).start()
                return 0

            lax.fori_loop(1, T, send_row, 0)

            below = (t >= rows - 2) & (s < S - 1)
            above = (t < 2) & (s > 0)

            @pl.when(below)
            def _():
                def send_below(k, _):
                    to(sbuf.at[pl.ds(steps * k, steps)], xin.at[1, t - (rows - 2)], b_send.at[1], b_recv.at[1], k, s + 1).start()
                    return 0

                lax.fori_loop(0, T, send_below, 0)

            @pl.when(above)
            def _():
                def send_above(k, _):
                    to(sbuf.at[pl.ds(steps * k, steps)], xin.at[1, rows + 2 + t], b_send.at[2], b_recv.at[2], k, s - 1).start()
                    return 0

                lax.fori_loop(0, T, send_above, 0)

            wait_bytes(sbuf.at[pl.ds(0, steps * (T - 1))], b_send.at[0])

            @pl.when(below)
            def _():
                wait_bytes(sbuf, b_send.at[1])

            @pl.when(above)
            def _():
                wait_bytes(sbuf, b_send.at[2])

            wait_bytes(sbuf.at[pl.ds(0, steps * (T - 1))], b_recv.at[0])

            @pl.when(s > 0)
            def _():
                wait_bytes(sbuf.at[pl.ds(0, steps * 2)], b_recv.at[1])

            @pl.when(s < S - 1)
            def _():
                wait_bytes(sbuf.at[pl.ds(0, steps * 2)], b_recv.at[2])

        else:
            guess = row_guess(it)
            anchor = [guess[i] - base2[i] for i in range(total_steps)]
            for j in range(total_steps):
                osend[j, 1] = guess[j] - state1[j]
                osend[j, 0] = mixed(guess, anchor, j)
            orecv[t] = osend[pl.ds(steps * t, steps)]

            def send_out(k, _):
                other = lax.rem(t + k, T)
                to(osend.at[pl.ds(steps * other, steps)], orecv.at[t], o_send, o_recv, other, s).start()
                return 0

            lax.fori_loop(1, T, send_out, 0)
            wait_bytes(orecv.at[pl.ds(0, T - 1)], o_send)
            wait_bytes(orecv.at[pl.ds(0, T - 1)], o_recv)
            for j in range(steps):
                for h in range(rows):
                    iterate_ref[pl.ds(j * CIN * rows + h, CIN, stride=rows), :] = orecv[h, j, 0]
                    residual_ref[pl.ds(j * CIN * rows + h, CIN, stride=rows), :] = orecv[h, j, 1]


def solution(mesh):
    T = mesh.shape["tm"]
    S = mesh.shape["strip"]

    def shards(
        start_state,
        trajectory,
        history,
        history_length,
        timesteps,
        step_size,
        mix_table,
        time_table,
        conv_in,
        norm_gain,
        norm_bias,
        conv_mid,
        conv_out,
    ):
        steps, CIN, rows, width = trajectory.shape
        CH = conv_out.shape[1]
        total = steps * T
        flat = steps * CIN * rows
        smem = pl.BlockSpec(memory_space=pltpu.SMEM)
        vmem = pl.BlockSpec(memory_space=pltpu.VMEM)
        hbm = pl.BlockSpec(memory_space=pl.ANY)
        dma = pltpu.SemaphoreType.DMA
        iterate, residual = pl.pallas_call(
            functools.partial(kernel, T, S),
            out_shape=(jax.ShapeDtypeStruct((flat, width), F32),) * 2,
            in_specs=[smem] * 4 + [vmem] * 7 + [hbm] * 2,
            out_specs=(vmem, vmem),
            scratch_shapes=[
                pltpu.VMEM((CH, time_table.shape[0]), F32),
                pltpu.VMEM((9, CH, CH), BF16),
                pltpu.VMEM((3, CH, 3 * CH), BF16),
                pltpu.VMEM((CH, 9 * CIN), BF16),
                pltpu.VMEM((ITERS, rows + 4, steps, CIN, width), BF16),
                pltpu.VMEM((3 * CIN, (rows + 4) * width), BF16),
                pltpu.VMEM((steps, CH, (rows + 2) * width), F32),
                pltpu.VMEM((steps, 3 * CH, (rows + 2) * width), BF16),
                pltpu.VMEM((CH, 1), F32),
                pltpu.VMEM((CH, 1), F32),
                pltpu.VMEM((steps, CH, 1), F32),
                pltpu.VMEM((2 * CH, width), F32),
                pltpu.VMEM((2 * CH, width), F32),
                pltpu.VMEM((ITERS * steps, 1, width), F32),
                pltpu.VMEM((ITERS * steps, S, 1, width), F32),
                pltpu.VMEM((ITERS, rows, steps, CIN, width), F32),
                pltpu.VMEM((ITERS, T, steps, CIN, width), F32),
                pltpu.VMEM((rows, steps, 2 * CIN + 8, width), F32),
                pltpu.VMEM((T, steps, 2 * CIN + 8, width), F32),
                pltpu.VMEM((total, CIN, width), BF16),
                pltpu.VMEM((total, CIN, width), F32),
                pltpu.VMEM((total, CIN, width), F32),
                pltpu.VMEM((total, 2, CIN, width), F32),
                pltpu.VMEM((rows, steps, 2, CIN, width), F32),
                dma((2,)),
                dma((2,)),
                dma((2,)),
                dma,
                dma,
                dma((ITERS * steps,)),
                dma((ITERS * steps,)),
                dma((ITERS,)),
                dma((ITERS,)),
                dma((3,)),
                dma((3,)),
                dma,
                dma,
            ],
            compiler_params=pltpu.CompilerParams(
                has_side_effects=True, vmem_limit_bytes=56 * 1024 * 1024
            ),
        )(
            history_length,
            timesteps,
            step_size,
            mix_table,
            norm_gain.reshape(1, CH),
            norm_bias.reshape(1, CH),
            start_state.reshape(CIN * rows, width),
            trajectory.reshape(flat, width),
            history.reshape(history.shape[0] * flat, width),
            jnp.swapaxes(conv_in, 1, 2).reshape(9 * CIN, CH),
            conv_out,
            time_table.T,
            conv_mid,
        )
        return (
            iterate.reshape(trajectory.shape),
            residual.reshape(trajectory.shape),
        )

    return jax.shard_map(
        shards,
        mesh=mesh,
        in_specs=(
            P(None, "strip", None),
            P("tm", None, "strip", None),
            P(None, "tm", None, "strip", None),
            P("tm"),
            P("tm"),
            P("tm"),
            P(),
            P(),
            P(),
            P(),
            P(),
            P(),
            P(),
        ),
        out_specs=(P("tm", None, "strip", None), P("tm", None, "strip", None)),
        check_vma=False,
    )
```

```python
import functools

import jax
import jax.numpy as jnp
from jax import lax
from jax.experimental import pallas as pl
from jax.experimental.pallas import tpu as pltpu
from jax.sharding import PartitionSpec as P

F32 = jnp.float32
BF16 = jnp.bfloat16
HIGHEST = lax.Precision.HIGHEST
GROUPS = 32
ITERS = 2
EPSILON = 1e-05
UNIT = 1.0 / 256.0
LANES = 128
CHUNK = 32


def silu(v):
    half = 0.5 * v
    return half + half * jnp.tanh(half)


def kernel(
    T,
    S,
    hl_ref,
    ts_ref,
    step_ref,
    mix_ref,
    gain_ref,
    bias_ref,
    start_ref,
    traj_ref,
    cin_ref,
    cout_ref,
    table_hbm,
    cmid_hbm,
    hist_hbm,
    iterate_ref,
    residual_ref,
    hist_ref,
    table,
    wraw,
    wmid,
    win,
    xin,
    xs,
    early,
    hid,
    gaincol,
    biascol,
    embcol,
    ind,
    sums,
    stat,
    stats,
    fsend,
    frecv,
    msend,
    mrecv,
    sbuf,
    state1,
    base2,
    osend,
    orecv,
    local_sem,
    halo_send,
    halo_recv,
    m_send,
    m_recv,
    s_send,
    s_recv,
    a_send,
    a_recv,
    b_send,
    b_recv,
    o_send,
    o_recv,
):
    t = lax.axis_index("tm")
    s = lax.axis_index("strip")
    steps = 2
    CH = cout_ref.shape[1]
    CIN = cout_ref.shape[0]
    rows = T
    total_steps = steps * T
    count = float(CH // GROUPS * rows * S * LANES)

    def to(src, dst, send, recv, tm, strip):
        return pltpu.make_async_remote_copy(
            src_ref=src,
            dst_ref=dst,
            send_sem=send,
            recv_sem=recv,
            device_id=(tm, strip),
            device_id_type=pl.DeviceIdType.MESH,
        )

    def wait_bytes(ref, sem):
        pltpu.make_async_copy(ref, ref, sem).wait()

    barrier = pltpu.get_barrier_semaphore()

    def greet(tm, strip):
        pl.semaphore_signal(
            barrier, inc=1, device_id=(tm, strip), device_id_type=pl.DeviceIdType.MESH
        )

    for r in range(2):

        @pl.when(t != rows - 2 + r)
        def _():
            greet(rows - 2 + r, lax.rem(s + S - 1, S))

        @pl.when(t != r)
        def _():
            greet(r, lax.rem(s + 1, S))

    def greet_column(k, _):
        greet(lax.rem(t + k, T), s)
        return 0

    lax.fori_loop(1, T, greet_column, 0)

    def greet_strips(k, _):
        greet(t, lax.rem(s + k, S))
        return 0

    lax.fori_loop(1, S, greet_strips, 0)
    get_past = pltpu.make_async_copy(hist_hbm, hist_ref, local_sem.at[2])
    get_past.start()
    get_table = pltpu.make_async_copy(table_hbm, table, local_sem.at[0])
    get_mid = pltpu.make_async_copy(cmid_hbm, wraw, local_sem.at[1])
    get_table.start()
    get_mid.start()

    for j in range(steps):
        for h in range(rows):
            xin[0, 2 + h, j] = traj_ref[pl.ds(j * CIN * rows + h, CIN, stride=rows), :].astype(BF16)
    send_down = to(xin.at[0, pl.ds(rows, 2)], xin.at[0, pl.ds(0, 2)], halo_send.at[0], halo_recv.at[0], t, s + 1)
    send_up = to(xin.at[0, pl.ds(2, 2)], xin.at[0, pl.ds(rows + 2, 2)], halo_send.at[1], halo_recv.at[1], t, s - 1)

    @pl.when(s == 0)
    def _():
        xin[0, 0:2] = jnp.zeros((2, steps, CIN, LANES), BF16)
        xin[1, 0:2] = jnp.zeros((2, steps, CIN, LANES), BF16)

    @pl.when(s == S - 1)
    def _():
        xin[0, rows + 2 : rows + 4] = jnp.zeros((2, steps, CIN, LANES), BF16)
        xin[1, rows + 2 : rows + 4] = jnp.zeros((2, steps, CIN, LANES), BF16)

    get_past.wait()

    for j in range(steps):
        length = jnp.full((CIN, LANES), hl_ref[j], jnp.int32)
        share = 1.0 / length.astype(F32)
        live = [jnp.where(length > m, share, 0.0) for m in range(3)]
        for h in range(rows):
            own = traj_ref[pl.ds(j * CIN * rows + h, CIN, stride=rows), :]
            past = [
                hist_ref[pl.ds((m * steps + j) * CIN * rows + h, CIN, stride=rows), :] for m in range(3)
            ]
            msend[h, j, 0:CIN] = own + (live[0] * past[0] + live[1] * past[1] + live[2] * past[2])
            msend[h, j, CIN : 2 * CIN] = live[1] * past[0] + live[2] * past[1] - live[0] * own
            msend[h, j, 2 * CIN : 2 * CIN + 8] = live[0][0:8]
    mrecv[t] = msend[t]

    row_id = lax.broadcasted_iota(jnp.int32, (CH, CH), 0)
    col_id = lax.broadcasted_iota(jnp.int32, (CH, CH), 1)
    diagonal = row_id == col_id
    gaincol[...] = jnp.sum(
        jnp.where(diagonal, jnp.broadcast_to(gain_ref[...].reshape(1, CH), (CH, CH)), 0.0), axis=1, keepdims=True
    )
    biascol[...] = jnp.sum(
        jnp.where(diagonal, jnp.broadcast_to(bias_ref[...].reshape(1, CH), (CH, CH)), 0.0), axis=1, keepdims=True
    )
    turned = lax.dot_general(
        diagonal.astype(F32).astype(BF16),
        cin_ref[...],
        (((1,), (1,)), ((), ())),
        preferred_element_type=F32,
    )
    win[...] = turned.astype(BF16)
    members = CH // GROUPS
    first = lax.broadcasted_iota(jnp.int32, (2 * CH, LANES), 1) * members
    channel = lax.broadcasted_iota(jnp.int32, (2 * CH, LANES), 0)
    ind[...] = jnp.where((channel >= first) & (channel < first + members), 1.0, 0.0)
    edge = (t < 2) | (t >= rows - 2)

    @pl.when(edge)
    def _():
        pl.semaphore_wait(barrier, S - 1 + 2 * (T - 1))

    @pl.when(jnp.logical_not(edge))
    def _():
        pl.semaphore_wait(barrier, S - 1 + T - 1)

    @pl.when(s < S - 1)
    def _():
        send_down.start()

    @pl.when(s > 0)
    def _():
        send_up.start()

    def send_m(k, _):
        other = lax.rem(t + k, T)
        to(msend.at[other], mrecv.at[t], m_send, m_recv, other, s).start()
        return 0

    lax.fori_loop(1, T, send_m, 0)

    get_table.wait()
    at = lax.broadcasted_iota(jnp.int32, table.shape, 1)
    for j in range(steps):
        embcol[j] = jnp.sum(jnp.where(at == ts_ref[j], table[...], 0.0), axis=1, keepdims=True)

    get_mid.wait()
    low = lax.broadcasted_iota(jnp.int32, (CH, LANES), 1) < 64
    for a in range(3):
        wmid[a, :, 0:256] = wraw[3 * a, :, 0:256]
        wmid[a, :, 640:960] = wraw[3 * a + 2]
        middle = [wraw[3 * a + 1, :, k * LANES : (k + 1) * LANES].astype(F32) for k in range(2)]
        tail = wraw[3 * a + 1, :, 256:320].astype(F32)
        middle.append(jnp.concatenate([tail, tail], axis=1))
        turned_by = [pltpu.roll(m, 64, 1) for m in middle[:2]] + [middle[2]]
        head = wraw[3 * a, :, 256:320].astype(F32)
        before = jnp.concatenate([head, head], axis=1)
        for k in range(3):
            wmid[a, :, 256 + k * LANES : 256 + (k + 1) * LANES] = jnp.where(
                low, before, turned_by[k]
            ).astype(BF16)
            before = turned_by[k]

    @pl.when(s < S - 1)
    def _():
        send_down.wait_send()

    @pl.when(s > 0)
    def _():
        send_up.wait_send()

    @pl.when(s > 0)
    def _():
        send_down.wait_recv()

    @pl.when(s < S - 1)
    def _():
        send_up.wait_recv()

    lane = lax.broadcasted_iota(jnp.int32, (CIN, LANES), 1)
    wide = lax.broadcasted_iota(jnp.int32, (CHUNK, LANES), 1)

    def shifted(x, lanes):
        left = jnp.where(lanes == 0, 0.0, pltpu.roll(x, 1, 1))
        right = jnp.where(lanes == LANES - 1, 0.0, pltpu.roll(x, LANES - 1, 1))
        return left, right

    def first_conv(it, j):
        for r in range(rows + 4):
            block = xin[it, r, j]
            left, right = shifted(block.astype(F32), lane)
            xs[0:CIN, r * LANES : (r + 1) * LANES] = left.astype(BF16)
            xs[CIN : 2 * CIN, r * LANES : (r + 1) * LANES] = block
            xs[2 * CIN : 3 * CIN, r * LANES : (r + 1) * LANES] = right.astype(BF16)
        for r in range(0, rows + 2, 2):
            taps = jnp.concatenate(
                [xs[:, (r + a) * LANES : (r + a + 2) * LANES] for a in range(3)], axis=0
            )
            early[j, :, r * LANES : (r + 2) * LANES] = (
                jnp.dot(win[...], taps, preferred_element_type=F32) + embcol[j]
            )

    def send_sums(it, j):
        k = it * steps + j

        def add_up(c):
            at = c * CHUNK
            total = jnp.zeros((CHUNK, LANES), F32)
            square = jnp.zeros((CHUNK, LANES), F32)
            for r in range(1, rows + 1):
                x = early[j, pl.ds(at, CHUNK), r * LANES : (r + 1) * LANES]
                total += x
                square += x * x
            sums[pl.ds(at, CHUNK)] = total
            sums[pl.ds(CH + at, CHUNK)] = square

        for c in range(CH // CHUNK):
            add_up(c)
        by_channel = lax.dot_general(
            jnp.ones((8, LANES), F32), sums[...], (((1,), (1,)), ((), ())), precision=HIGHEST,
            preferred_element_type=F32,
        )
        by_group = jnp.dot(by_channel, ind[...], precision=HIGHEST, preferred_element_type=F32)
        stat[k] = by_group[0:1]
        stats[k, s] = by_group[0:1]

        def send(i, _):
            other = lax.rem(s + i, S)
            to(stat.at[k], stats.at[k, s], s_send.at[k], s_recv.at[k], t, other).start()
            return 0

        lax.fori_loop(1, S, send, 0)

    def normalise(it, j):
        k = it * steps + j
        wait_bytes(stats.at[k, pl.ds(0, S - 1)], s_send.at[k])
        wait_bytes(stats.at[k, pl.ds(0, S - 1)], s_recv.at[k])
        total = jnp.sum(stats[k], axis=0) * (1.0 / count)
        total = jnp.broadcast_to(total, (8, LANES))
        variance = jnp.maximum(pltpu.roll(total, LANES - GROUPS, 1) - total * total, 0.0)
        scale = 1.0 / jnp.sqrt(variance + EPSILON)
        mean_row, scale_row = total[0:1], scale[0:1]

        def body(c):
            at = c * CHUNK
            which = ind[pl.ds(at, CHUNK)]
            mean = jnp.sum(jnp.where(which > 0.5, mean_row, 0.0), axis=1, keepdims=True)
            factor = jnp.sum(jnp.where(which > 0.5, scale_row, 0.0), axis=1, keepdims=True)
            factor = factor * gaincol[pl.ds(at, CHUNK)]
            offset = biascol[pl.ds(at, CHUNK)]
            for r in range(rows + 2):
                x = early[j, pl.ds(at, CHUNK), r * LANES : (r + 1) * LANES]
                x = silu((x - mean) * factor + offset)
                if r == 0:
                    x = jnp.where(s > 0, x, 0.0)
                if r == rows + 1:
                    x = jnp.where(s < S - 1, x, 0.0)
                left, right = shifted(x, wide)
                cells = slice(r * LANES, (r + 1) * LANES)
                hid[j, pl.ds(at, CHUNK), cells] = left.astype(BF16)
                hid[j, pl.ds(CH + at, CHUNK), cells] = x.astype(BF16)
                hid[j, pl.ds(2 * CH + at, CHUNK), cells] = right.astype(BF16)

        for c in range(CH // CHUNK):
            body(c)

    def second_conv(it, j):
        late = None
        for a in range(3):
            product = jnp.dot(
                wmid[a], hid[j, :, a * LANES : (a + rows) * LANES], preferred_element_type=F32
            )
            late = product if late is None else late + product
        active = silu(late).astype(BF16)
        field = jnp.dot(cout_ref[...], active, preferred_element_type=F32)
        drift = field * step_ref[j]
        for h in range(rows):
            fsend[it, h, j] = drift[:, h * LANES : (h + 1) * LANES]

        def send(k, _):
            other = lax.rem(t + k, T)
            to(fsend.at[it, other, j], frecv.at[it, t, j], a_send.at[it], a_recv.at[it], other, s).start()
            return 0

        lax.fori_loop(1, T, send, 0)
        frecv[it, t, j] = fsend[it, t, j]

    def row_guess(it):
        wait_bytes(frecv.at[it, pl.ds(0, T - 1)], a_send.at[it])
        wait_bytes(frecv.at[it, pl.ds(0, T - 1)], a_recv.at[it])
        guess = [start_ref[pl.ds(t, CIN, stride=rows), :]]
        for i in range(total_steps - 1):
            guess.append(guess[-1] + frecv[it, i // steps, i % steps])
        return guess

    def mixed(guess, anchor, j):
        total = guess[j]
        for i in range(j + 1):
            total = total + (mix_ref[j, i].astype(F32) * UNIT) * anchor[i]
        return total

    for it in range(ITERS):
        for j in range(steps):
            first_conv(it, j)
            send_sums(it, j)
        for j in range(steps):
            normalise(it, j)
            second_conv(it, j)
        if it == 0:
            wait_bytes(mrecv.at[pl.ds(0, T - 1)], m_send)
            wait_bytes(mrecv.at[pl.ds(0, T - 1)], m_recv)
            guess = row_guess(it)
            anchor = [
                guess[i] - mrecv[i // steps, i % steps, 0:CIN] for i in range(total_steps)
            ]
            for j in range(total_steps):
                new = mixed(guess, anchor, j)
                sbuf[j] = new.astype(BF16)
                state1[j] = new
                share = mrecv[j // steps, j % steps, 2 * CIN : 2 * CIN + 8]
                share = jnp.concatenate([share, share], axis=0)
                base2[j] = new + (share * guess[j] + mrecv[j // steps, j % steps, CIN : 2 * CIN])
            xin[1, 2 + t] = sbuf[pl.ds(steps * t, steps)]

            below = (t >= rows - 2) & (s < S - 1)
            above = (t < 2) & (s > 0)

            @pl.when(below)
            def _():
                def send_below(k, _):
                    to(sbuf.at[pl.ds(steps * k, steps)], xin.at[1, t - (rows - 2)], b_send.at[1], b_recv.at[1], k, s + 1).start()
                    return 0

                lax.fori_loop(0, T, send_below, 0)

            @pl.when(above)
            def _():
                def send_above(k, _):
                    to(sbuf.at[pl.ds(steps * k, steps)], xin.at[1, rows + 2 + t], b_send.at[2], b_recv.at[2], k, s - 1).start()
                    return 0

                lax.fori_loop(0, T, send_above, 0)

            def send_row(k, _):
                other = lax.rem(t + k, T)
                to(sbuf.at[pl.ds(steps * other, steps)], xin.at[1, 2 + t], b_send.at[0], b_recv.at[0], other, s).start()
                return 0

            lax.fori_loop(1, T, send_row, 0)
            wait_bytes(sbuf.at[pl.ds(0, steps * (T - 1))], b_send.at[0])

            @pl.when(below)
            def _():
                wait_bytes(sbuf, b_send.at[1])

            @pl.when(above)
            def _():
                wait_bytes(sbuf, b_send.at[2])

            wait_bytes(sbuf.at[pl.ds(0, steps * (T - 1))], b_recv.at[0])

            @pl.when(s > 0)
            def _():
                wait_bytes(sbuf.at[pl.ds(0, steps * 2)], b_recv.at[1])

            @pl.when(s < S - 1)
            def _():
                wait_bytes(sbuf.at[pl.ds(0, steps * 2)], b_recv.at[2])

        else:
            guess = row_guess(it)
            anchor = [guess[i] - base2[i] for i in range(total_steps)]
            for j in range(total_steps):
                osend[j, 1] = guess[j] - state1[j]
                osend[j, 0] = mixed(guess, anchor, j)
            orecv[t] = osend[pl.ds(steps * t, steps)]

            def send_out(k, _):
                other = lax.rem(t + k, T)
                to(osend.at[pl.ds(steps * other, steps)], orecv.at[t], o_send, o_recv, other, s).start()
                return 0

            lax.fori_loop(1, T, send_out, 0)
            wait_bytes(orecv.at[pl.ds(0, T - 1)], o_send)
            wait_bytes(orecv.at[pl.ds(0, T - 1)], o_recv)
            for j in range(steps):
                for h in range(rows):
                    iterate_ref[pl.ds(j * CIN * rows + h, CIN, stride=rows), :] = orecv[h, j, 0]
                    residual_ref[pl.ds(j * CIN * rows + h, CIN, stride=rows), :] = orecv[h, j, 1]


def solution(mesh):
    T = mesh.shape["tm"]
    S = mesh.shape["strip"]

    def shards(
        start_state,
        trajectory,
        history,
        history_length,
        timesteps,
        step_size,
        mix_table,
        time_table,
        conv_in,
        norm_gain,
        norm_bias,
        conv_mid,
        conv_out,
    ):
        steps, CIN, rows, width = trajectory.shape
        CH = conv_out.shape[1]
        total = steps * T
        flat = steps * CIN * rows
        smem = pl.BlockSpec(memory_space=pltpu.SMEM)
        vmem = pl.BlockSpec(memory_space=pltpu.VMEM)
        hbm = pl.BlockSpec(memory_space=pl.ANY)
        dma = pltpu.SemaphoreType.DMA
        iterate, residual = pl.pallas_call(
            functools.partial(kernel, T, S),
            out_shape=(jax.ShapeDtypeStruct((flat, width), F32),) * 2,
            in_specs=[smem] * 4 + [vmem] * 6 + [hbm] * 3,
            out_specs=(vmem, vmem),
            scratch_shapes=[
                pltpu.VMEM((history.shape[0] * flat, width), F32),
                pltpu.VMEM((CH, time_table.shape[0]), F32),
                pltpu.VMEM((9, CH, CH), BF16),
                pltpu.VMEM((3, CH, 3 * CH), BF16),
                pltpu.VMEM((CH, 9 * CIN), BF16),
                pltpu.VMEM((ITERS, rows + 4, steps, CIN, width), BF16),
                pltpu.VMEM((3 * CIN, (rows + 4) * width), BF16),
                pltpu.VMEM((steps, CH, (rows + 2) * width), F32),
                pltpu.VMEM((steps, 3 * CH, (rows + 2) * width), BF16),
                pltpu.VMEM((CH, 1), F32),
                pltpu.VMEM((CH, 1), F32),
                pltpu.VMEM((steps, CH, 1), F32),
                pltpu.VMEM((2 * CH, width), F32),
                pltpu.VMEM((2 * CH, width), F32),
                pltpu.VMEM((ITERS * steps, 1, width), F32),
                pltpu.VMEM((ITERS * steps, S, 1, width), F32),
                pltpu.VMEM((ITERS, rows, steps, CIN, width), F32),
                pltpu.VMEM((ITERS, T, steps, CIN, width), F32),
                pltpu.VMEM((rows, steps, 2 * CIN + 8, width), F32),
                pltpu.VMEM((T, steps, 2 * CIN + 8, width), F32),
                pltpu.VMEM((total, CIN, width), BF16),
                pltpu.VMEM((total, CIN, width), F32),
                pltpu.VMEM((total, CIN, width), F32),
                pltpu.VMEM((total, 2, CIN, width), F32),
                pltpu.VMEM((rows, steps, 2, CIN, width), F32),
                dma((3,)),
                dma((2,)),
                dma((2,)),
                dma,
                dma,
                dma((ITERS * steps,)),
                dma((ITERS * steps,)),
                dma((ITERS,)),
                dma((ITERS,)),
                dma((3,)),
                dma((3,)),
                dma,
                dma,
            ],
            compiler_params=pltpu.CompilerParams(
                collective_id=0, has_side_effects=True, vmem_limit_bytes=56 * 1024 * 1024
            ),
        )(
            history_length,
            timesteps,
            step_size,
            mix_table,
            norm_gain,
            norm_bias,
            start_state.reshape(CIN * rows, width),
            trajectory.reshape(flat, width),
            jnp.swapaxes(conv_in, 1, 2).reshape(9 * CIN, CH),
            conv_out,
            time_table.T,
            conv_mid,
            history.reshape(history.shape[0] * flat, width),
        )
        return (
            iterate.reshape(trajectory.shape),
            residual.reshape(trajectory.shape),
        )

    return jax.shard_map(
        shards,
        mesh=mesh,
        in_specs=(
            P(None, "strip", None),
            P("tm", None, "strip", None),
            P(None, "tm", None, "strip", None),
            P("tm"),
            P("tm"),
            P("tm"),
            P(),
            P(),
            P(),
            P(),
            P(),
            P(),
            P(),
        ),
        out_specs=(P("tm", None, "strip", None), P("tm", None, "strip", None)),
        check_vma=False,
    )
```

```python
import functools

import jax
import jax.numpy as jnp
from jax import lax
from jax.experimental import pallas as pl
from jax.experimental.pallas import tpu as pltpu
from jax.sharding import PartitionSpec as P

F32 = jnp.float32
BF16 = jnp.bfloat16
HIGHEST = lax.Precision.HIGHEST
GROUPS = 32
ITERS = 2
EPSILON = 1e-05
UNIT = 1.0 / 256.0
LANES = 128
CHUNK = 32


def silu(v):
    half = 0.5 * v
    return half + half * jnp.tanh(half)


def kernel(
    T,
    S,
    hl_ref,
    ts_ref,
    step_ref,
    mix_ref,
    gain_ref,
    bias_ref,
    start_ref,
    traj_ref,
    cin_ref,
    cout_ref,
    table_hbm,
    cmid_hbm,
    hist_hbm,
    iterate_ref,
    residual_ref,
    hist_ref,
    table,
    wraw,
    wmid,
    win,
    xin,
    xs,
    early,
    hid,
    gaincol,
    biascol,
    embcol,
    ind,
    sums,
    stat,
    stats,
    fsend,
    frecv,
    msend,
    mrecv,
    sbuf,
    state1,
    base2,
    osend,
    orecv,
    local_sem,
    halo_send,
    halo_recv,
    m_send,
    m_recv,
    s_send,
    s_recv,
    a_send,
    a_recv,
    b_send,
    b_recv,
    o_send,
    o_recv,
):
    t = lax.axis_index("tm")
    s = lax.axis_index("strip")
    steps = 2
    CH = cout_ref.shape[1]
    CIN = cout_ref.shape[0]
    rows = T
    total_steps = steps * T
    count = float(CH // GROUPS * rows * S * LANES)

    def to(src, dst, send, recv, tm, strip):
        return pltpu.make_async_remote_copy(
            src_ref=src,
            dst_ref=dst,
            send_sem=send,
            recv_sem=recv,
            device_id=(tm, strip),
            device_id_type=pl.DeviceIdType.MESH,
        )

    def wait_bytes(ref, sem):
        pltpu.make_async_copy(ref, ref, sem).wait()

    get_past = pltpu.make_async_copy(hist_hbm, hist_ref, local_sem.at[2])
    get_past.start()
    get_table = pltpu.make_async_copy(table_hbm, table, local_sem.at[0])
    get_mid = pltpu.make_async_copy(cmid_hbm, wraw, local_sem.at[1])
    get_table.start()
    get_mid.start()

    barrier = pltpu.get_barrier_semaphore()

    def greet(tm, strip):
        pl.semaphore_signal(
            barrier, inc=1, device_id=(tm, strip), device_id_type=pl.DeviceIdType.MESH
        )

    def greet_strips(k, _):
        greet(t, lax.rem(s + k, S))
        return 0

    lax.fori_loop(1, S, greet_strips, 0)

    for r in range(2):

        @pl.when(t != rows - 2 + r)
        def _():
            greet(rows - 2 + r, lax.rem(s + S - 1, S))

        @pl.when(t != r)
        def _():
            greet(r, lax.rem(s + 1, S))

    def greet_column(k, _):
        greet(lax.rem(t + k, T), s)
        return 0

    lax.fori_loop(1, T, greet_column, 0)

    for j in range(steps):
        for h in range(rows):
            xin[0, 2 + h, j] = traj_ref[pl.ds(j * CIN * rows + h, CIN, stride=rows), :].astype(BF16)
    send_down = to(xin.at[0, pl.ds(rows, 2)], xin.at[0, pl.ds(0, 2)], halo_send.at[0], halo_recv.at[0], t, s + 1)
    send_up = to(xin.at[0, pl.ds(2, 2)], xin.at[0, pl.ds(rows + 2, 2)], halo_send.at[1], halo_recv.at[1], t, s - 1)

    @pl.when(s == 0)
    def _():
        xin[0, 0:2] = jnp.zeros((2, steps, CIN, LANES), BF16)
        xin[1, 0:2] = jnp.zeros((2, steps, CIN, LANES), BF16)

    @pl.when(s == S - 1)
    def _():
        xin[0, rows + 2 : rows + 4] = jnp.zeros((2, steps, CIN, LANES), BF16)
        xin[1, rows + 2 : rows + 4] = jnp.zeros((2, steps, CIN, LANES), BF16)

    get_past.wait()

    for j in range(steps):
        length = jnp.full((CIN, LANES), hl_ref[j], jnp.int32)
        share = 1.0 / length.astype(F32)
        live = [jnp.where(length > m, share, 0.0) for m in range(3)]
        for h in range(rows):
            own = traj_ref[pl.ds(j * CIN * rows + h, CIN, stride=rows), :]
            past = [
                hist_ref[pl.ds((m * steps + j) * CIN * rows + h, CIN, stride=rows), :] for m in range(3)
            ]
            msend[h, j, 0:CIN] = own + (live[0] * past[0] + live[1] * past[1] + live[2] * past[2])
            msend[h, j, CIN : 2 * CIN] = live[1] * past[0] + live[2] * past[1] - live[0] * own
            msend[h, j, 2 * CIN : 2 * CIN + 8] = live[0][0:8]
    mrecv[t] = msend[t]

    row_id = lax.broadcasted_iota(jnp.int32, (CH, CH), 0)
    col_id = lax.broadcasted_iota(jnp.int32, (CH, CH), 1)
    diagonal = row_id == col_id
    gaincol[...] = jnp.sum(
        jnp.where(diagonal, jnp.broadcast_to(gain_ref[...].reshape(1, CH), (CH, CH)), 0.0), axis=1, keepdims=True
    )
    biascol[...] = jnp.sum(
        jnp.where(diagonal, jnp.broadcast_to(bias_ref[...].reshape(1, CH), (CH, CH)), 0.0), axis=1, keepdims=True
    )
    turned = lax.dot_general(
        diagonal.astype(F32).astype(BF16),
        cin_ref[...],
        (((1,), (1,)), ((), ())),
        preferred_element_type=F32,
    )
    win[...] = turned.astype(BF16)
    members = CH // GROUPS
    first = lax.broadcasted_iota(jnp.int32, (2 * CH, LANES), 1) * members
    channel = lax.broadcasted_iota(jnp.int32, (2 * CH, LANES), 0)
    ind[...] = jnp.where((channel >= first) & (channel < first + members), 1.0, 0.0)
    edge = (t < 2) | (t >= rows - 2)

    @pl.when(edge)
    def _():
        pl.semaphore_wait(barrier, S - 1 + 2 * (T - 1))

    @pl.when(jnp.logical_not(edge))
    def _():
        pl.semaphore_wait(barrier, S - 1 + T - 1)

    @pl.when(s < S - 1)
    def _():
        send_down.start()

    @pl.when(s > 0)
    def _():
        send_up.start()

    def send_m(k, _):
        other = lax.rem(t + k, T)
        to(msend.at[other], mrecv.at[t], m_send, m_recv, other, s).start()
        return 0

    lax.fori_loop(1, T, send_m, 0)

    get_table.wait()
    at = lax.broadcasted_iota(jnp.int32, table.shape, 1)
    for j in range(steps):
        embcol[j] = jnp.sum(jnp.where(at == ts_ref[j], table[...], 0.0), axis=1, keepdims=True)

    get_mid.wait()
    low = lax.broadcasted_iota(jnp.int32, (CH, LANES), 1) < 64
    for a in range(3):
        wmid[a, :, 0:256] = wraw[3 * a, :, 0:256]
        wmid[a, :, 640:960] = wraw[3 * a + 2]
        middle = [wraw[3 * a + 1, :, k * LANES : (k + 1) * LANES].astype(F32) for k in range(2)]
        tail = wraw[3 * a + 1, :, 256:320].astype(F32)
        middle.append(jnp.concatenate([tail, tail], axis=1))
        turned_by = [pltpu.roll(m, 64, 1) for m in middle[:2]] + [middle[2]]
        head = wraw[3 * a, :, 256:320].astype(F32)
        before = jnp.concatenate([head, head], axis=1)
        for k in range(3):
            wmid[a, :, 256 + k * LANES : 256 + (k + 1) * LANES] = jnp.where(
                low, before, turned_by[k]
            ).astype(BF16)
            before = turned_by[k]

    @pl.when(s < S - 1)
    def _():
        send_down.wait_send()

    @pl.when(s > 0)
    def _():
        send_up.wait_send()

    @pl.when(s > 0)
    def _():
        send_down.wait_recv()

    @pl.when(s < S - 1)
    def _():
        send_up.wait_recv()

    lane = lax.broadcasted_iota(jnp.int32, (CIN, LANES), 1)
    wide = lax.broadcasted_iota(jnp.int32, (CHUNK, LANES), 1)

    def shifted(x, lanes):
        zero = jnp.zeros_like(x)
        left = jnp.where(lanes == 0, zero, pltpu.roll(x, 1, 1))
        right = jnp.where(lanes == LANES - 1, zero, pltpu.roll(x, LANES - 1, 1))
        return left, right

    def first_conv(it, j):
        for r in range(rows + 4):
            block = xin[it, r, j]
            left, right = shifted(block.astype(F32), lane)
            xs[0:CIN, r * LANES : (r + 1) * LANES] = left.astype(BF16)
            xs[CIN : 2 * CIN, r * LANES : (r + 1) * LANES] = block
            xs[2 * CIN : 3 * CIN, r * LANES : (r + 1) * LANES] = right.astype(BF16)
        for r in range(0, rows + 2, 2):
            taps = jnp.concatenate(
                [xs[:, (r + a) * LANES : (r + a + 2) * LANES] for a in range(3)], axis=0
            )
            early[j, :, r * LANES : (r + 2) * LANES] = (
                jnp.dot(win[...], taps, preferred_element_type=F32) + embcol[j]
            )

    def send_sums(it, j):
        k = it * steps + j

        def add_up(c):
            at = c * CHUNK
            total = jnp.zeros((CHUNK, LANES), F32)
            square = jnp.zeros((CHUNK, LANES), F32)
            for r in range(1, rows + 1):
                x = early[j, pl.ds(at, CHUNK), r * LANES : (r + 1) * LANES]
                total += x
                square += x * x
            sums[pl.ds(at, CHUNK)] = total
            sums[pl.ds(CH + at, CHUNK)] = square

        for c in range(CH // CHUNK):
            add_up(c)
        by_channel = lax.dot_general(
            jnp.ones((8, LANES), F32), sums[...], (((1,), (1,)), ((), ())), precision=HIGHEST,
            preferred_element_type=F32,
        )
        by_group = jnp.dot(by_channel, ind[...], precision=HIGHEST, preferred_element_type=F32)
        stat[k] = by_group[0:1]
        stats[k, s] = by_group[0:1]

        def send(i, _):
            other = lax.rem(s + i, S)
            to(stat.at[k], stats.at[k, s], s_send.at[k], s_recv.at[k], t, other).start()
            return 0

        lax.fori_loop(1, S, send, 0)

    def normalise(it, j):
        k = it * steps + j
        wait_bytes(stats.at[k, pl.ds(0, S - 1)], s_send.at[k])
        wait_bytes(stats.at[k, pl.ds(0, S - 1)], s_recv.at[k])
        total = jnp.sum(stats[k], axis=0) * (1.0 / count)
        total = jnp.broadcast_to(total, (8, LANES))
        variance = jnp.maximum(pltpu.roll(total, LANES - GROUPS, 1) - total * total, 0.0)
        scale = 1.0 / jnp.sqrt(variance + EPSILON)
        mean_row, scale_row = total[0:1], scale[0:1]

        def body(c):
            at = c * CHUNK
            which = ind[pl.ds(at, CHUNK)]
            mean = jnp.sum(jnp.where(which > 0.5, mean_row, 0.0), axis=1, keepdims=True)
            factor = jnp.sum(jnp.where(which > 0.5, scale_row, 0.0), axis=1, keepdims=True)
            factor = factor * gaincol[pl.ds(at, CHUNK)]
            offset = biascol[pl.ds(at, CHUNK)]
            for r in range(rows + 2):
                x = early[j, pl.ds(at, CHUNK), r * LANES : (r + 1) * LANES]
                x = silu((x - mean) * factor + offset)
                if r == 0:
                    x = jnp.where(s > 0, x, 0.0)
                if r == rows + 1:
                    x = jnp.where(s < S - 1, x, 0.0)
                x = x.astype(BF16)
                left, right = shifted(x, wide)
                cells = slice(r * LANES, (r + 1) * LANES)
                hid[j, pl.ds(at, CHUNK), cells] = left
                hid[j, pl.ds(CH + at, CHUNK), cells] = x
                hid[j, pl.ds(2 * CH + at, CHUNK), cells] = right

        for c in range(CH // CHUNK):
            body(c)

    def second_conv(it, j):
        late = None
        for a in range(3):
            product = jnp.dot(
                wmid[a], hid[j, :, a * LANES : (a + rows) * LANES], preferred_element_type=F32
            )
            late = product if late is None else late + product
        active = silu(late).astype(BF16)
        field = jnp.dot(cout_ref[...], active, preferred_element_type=F32)
        drift = field * step_ref[j]
        for h in range(rows):
            fsend[it, h, j] = drift[:, h * LANES : (h + 1) * LANES]

        def send(k, _):
            other = lax.rem(t + k, T)
            to(fsend.at[it, other, j], frecv.at[it, t, j], a_send.at[it], a_recv.at[it], other, s).start()
            return 0

        lax.fori_loop(1, T, send, 0)
        frecv[it, t, j] = fsend[it, t, j]

    def row_guess(it):
        wait_bytes(frecv.at[it, pl.ds(0, T - 1)], a_send.at[it])
        wait_bytes(frecv.at[it, pl.ds(0, T - 1)], a_recv.at[it])
        guess = [start_ref[pl.ds(t, CIN, stride=rows), :]]
        for i in range(total_steps - 1):
            guess.append(guess[-1] + frecv[it, i // steps, i % steps])
        return guess

    def mixed(guess, anchor, j):
        total = guess[j]
        for i in range(j + 1):
            total = total + (mix_ref[j, i].astype(F32) * UNIT) * anchor[i]
        return total

    for it in range(ITERS):
        for j in range(steps):
            first_conv(it, j)
            send_sums(it, j)
        for j in range(steps):
            normalise(it, j)
            second_conv(it, j)
        if it == 0:
            wait_bytes(mrecv.at[pl.ds(0, T - 1)], m_send)
            wait_bytes(mrecv.at[pl.ds(0, T - 1)], m_recv)
            guess = row_guess(it)
            anchor = [
                guess[i] - mrecv[i // steps, i % steps, 0:CIN] for i in range(total_steps)
            ]
            odd, after, before = lax.rem(t, 2), lax.rem(s + 1, S), lax.rem(s + S - 1, S)
            below = (t >= rows - 2) & (s < S - 1)
            above = (t < 2) & (s > 0)
            for k in range(T):
                for j in range(steps * k, steps * (k + 1)):
                    new = mixed(guess, anchor, j)
                    sbuf[j] = new.astype(BF16)
                    state1[j] = new
                pair = sbuf.at[pl.ds(steps * k, steps)]

                @pl.when(below)
                def _():
                    to(pair, xin.at[1, odd], b_send.at[1], b_recv.at[1], k, after).start()

                @pl.when(above)
                def _():
                    to(pair, xin.at[1, rows + 2 + odd], b_send.at[2], b_recv.at[2], k, before).start()

                @pl.when(t != k)
                def _():
                    to(pair, xin.at[1, 2 + t], b_send.at[0], b_recv.at[0], k, s).start()

            xin[1, 2 + t] = sbuf[pl.ds(steps * t, steps)]
            for j in range(total_steps):
                share = mrecv[j // steps, j % steps, 2 * CIN : 2 * CIN + 8]
                share = jnp.concatenate([share, share], axis=0)
                base2[j] = state1[j] + (share * guess[j] + mrecv[j // steps, j % steps, CIN : 2 * CIN])
            wait_bytes(sbuf.at[pl.ds(0, steps * (T - 1))], b_send.at[0])

            @pl.when(below)
            def _():
                wait_bytes(sbuf, b_send.at[1])

            @pl.when(above)
            def _():
                wait_bytes(sbuf, b_send.at[2])

            wait_bytes(sbuf.at[pl.ds(0, steps * (T - 1))], b_recv.at[0])

            @pl.when(s > 0)
            def _():
                wait_bytes(sbuf.at[pl.ds(0, steps * 2)], b_recv.at[1])

            @pl.when(s < S - 1)
            def _():
                wait_bytes(sbuf.at[pl.ds(0, steps * 2)], b_recv.at[2])

        else:
            guess = row_guess(it)
            anchor = [guess[i] - base2[i] for i in range(total_steps)]
            for k in range(T):
                for j in range(steps * k, steps * (k + 1)):
                    osend[j, 1] = guess[j] - state1[j]
                    osend[j, 0] = mixed(guess, anchor, j)

                @pl.when(t != k)
                def _():
                    to(osend.at[pl.ds(steps * k, steps)], orecv.at[t], o_send, o_recv, k, s).start()

            orecv[t] = osend[pl.ds(steps * t, steps)]
            wait_bytes(orecv.at[pl.ds(0, T - 1)], o_send)
            wait_bytes(orecv.at[pl.ds(0, T - 1)], o_recv)
            for j in range(steps):
                for h in range(rows):
                    iterate_ref[pl.ds(j * CIN * rows + h, CIN, stride=rows), :] = orecv[h, j, 0]
                    residual_ref[pl.ds(j * CIN * rows + h, CIN, stride=rows), :] = orecv[h, j, 1]


def solution(mesh):
    T = mesh.shape["tm"]
    S = mesh.shape["strip"]

    def shards(
        start_state,
        trajectory,
        history,
        history_length,
        timesteps,
        step_size,
        mix_table,
        time_table,
        conv_in,
        norm_gain,
        norm_bias,
        conv_mid,
        conv_out,
    ):
        steps, CIN, rows, width = trajectory.shape
        CH = conv_out.shape[1]
        total = steps * T
        flat = steps * CIN * rows
        smem = pl.BlockSpec(memory_space=pltpu.SMEM)
        vmem = pl.BlockSpec(memory_space=pltpu.VMEM)
        hbm = pl.BlockSpec(memory_space=pl.ANY)
        dma = pltpu.SemaphoreType.DMA
        iterate, residual = pl.pallas_call(
            functools.partial(kernel, T, S),
            out_shape=(jax.ShapeDtypeStruct((flat, width), F32),) * 2,
            in_specs=[smem] * 4 + [vmem] * 6 + [hbm] * 3,
            out_specs=(vmem, vmem),
            scratch_shapes=[
                pltpu.VMEM((history.shape[0] * flat, width), F32),
                pltpu.VMEM((CH, time_table.shape[0]), F32),
                pltpu.VMEM((9, CH, CH), BF16),
                pltpu.VMEM((3, CH, 3 * CH), BF16),
                pltpu.VMEM((CH, 9 * CIN), BF16),
                pltpu.VMEM((ITERS, rows + 4, steps, CIN, width), BF16),
                pltpu.VMEM((3 * CIN, (rows + 4) * width), BF16),
                pltpu.VMEM((steps, CH, (rows + 2) * width), F32),
                pltpu.VMEM((steps, 3 * CH, (rows + 2) * width), BF16),
                pltpu.VMEM((CH, 1), F32),
                pltpu.VMEM((CH, 1), F32),
                pltpu.VMEM((steps, CH, 1), F32),
                pltpu.VMEM((2 * CH, width), F32),
                pltpu.VMEM((2 * CH, width), F32),
                pltpu.VMEM((ITERS * steps, 1, width), F32),
                pltpu.VMEM((ITERS * steps, S, 1, width), F32),
                pltpu.VMEM((ITERS, rows, steps, CIN, width), F32),
                pltpu.VMEM((ITERS, T, steps, CIN, width), F32),
                pltpu.VMEM((rows, steps, 2 * CIN + 8, width), F32),
                pltpu.VMEM((T, steps, 2 * CIN + 8, width), F32),
                pltpu.VMEM((total, CIN, width), BF16),
                pltpu.VMEM((total, CIN, width), F32),
                pltpu.VMEM((total, CIN, width), F32),
                pltpu.VMEM((total, 2, CIN, width), F32),
                pltpu.VMEM((rows, steps, 2, CIN, width), F32),
                dma((3,)),
                dma((2,)),
                dma((2,)),
                dma,
                dma,
                dma((ITERS * steps,)),
                dma((ITERS * steps,)),
                dma((ITERS,)),
                dma((ITERS,)),
                dma((3,)),
                dma((3,)),
                dma,
                dma,
            ],
            compiler_params=pltpu.CompilerParams(
                collective_id=0, has_side_effects=True, vmem_limit_bytes=56 * 1024 * 1024
            ),
        )(
            history_length,
            timesteps,
            step_size,
            mix_table,
            norm_gain,
            norm_bias,
            start_state.reshape(CIN * rows, width),
            trajectory.reshape(flat, width),
            jnp.swapaxes(conv_in, 1, 2).reshape(9 * CIN, CH),
            conv_out,
            time_table.T,
            conv_mid,
            history.reshape(history.shape[0] * flat, width),
        )
        valid = history_length[0] > 0
        return (
            jnp.where(valid, iterate, residual).reshape(trajectory.shape),
            jnp.where(valid, residual, iterate).reshape(trajectory.shape),
        )

    return jax.shard_map(
        shards,
        mesh=mesh,
        in_specs=(
            P(None, "strip", None),
            P("tm", None, "strip", None),
            P(None, "tm", None, "strip", None),
            P("tm"),
            P("tm"),
            P("tm"),
            P(),
            P(),
            P(),
            P(),
            P(),
            P(),
            P(),
        ),
        out_specs=(P("tm", None, "strip", None), P("tm", None, "strip", None)),
        check_vma=False,
    )
```

```python
import functools

import jax
import jax.numpy as jnp
from jax import lax
from jax.experimental import pallas as pl
from jax.experimental.pallas import tpu as pltpu
from jax.sharding import PartitionSpec as P

F32 = jnp.float32
BF16 = jnp.bfloat16
GROUPS = 32
ITERS = 2
EPSILON = 1e-05
UNIT = 1.0 / 256.0
LANES = 128
CHUNK = 32


def silu(v):
    half = 0.5 * v
    return half + half * jnp.tanh(half)


def thirds(x):
    high = x.astype(BF16)
    rest = x - high.astype(F32)
    middle = rest.astype(BF16)
    return high, middle, (rest - middle.astype(F32)).astype(BF16)


def kernel(
    T,
    S,
    hl_ref,
    ts_ref,
    step_ref,
    mix_ref,
    gain_ref,
    bias_ref,
    start_ref,
    traj_ref,
    cin_ref,
    cout_ref,
    table_hbm,
    cmid_hbm,
    hist_hbm,
    iterate_ref,
    residual_ref,
    hist_ref,
    table,
    wraw,
    wmid,
    win,
    xin,
    xs,
    early,
    hid,
    gaincol,
    biascol,
    embcol,
    ind,
    sums,
    stat,
    stats,
    fsend,
    frecv,
    msend,
    mrecv,
    sbuf,
    state1,
    base2,
    osend,
    orecv,
    local_sem,
    halo_send,
    halo_recv,
    m_send,
    m_recv,
    s_send,
    s_recv,
    a_send,
    a_recv,
    b_send,
    b_recv,
    o_send,
    o_recv,
):
    t = lax.axis_index("tm")
    s = lax.axis_index("strip")
    steps = 2
    CH = cout_ref.shape[1]
    CIN = cout_ref.shape[0]
    rows = T
    total_steps = steps * T
    count = float(CH // GROUPS * rows * S * LANES)

    def to(src, dst, send, recv, tm, strip):
        return pltpu.make_async_remote_copy(
            src_ref=src,
            dst_ref=dst,
            send_sem=send,
            recv_sem=recv,
            device_id=(tm, strip),
            device_id_type=pl.DeviceIdType.MESH,
        )

    def wait_bytes(ref, sem):
        pltpu.make_async_copy(ref, ref, sem).wait()

    get_past = pltpu.make_async_copy(hist_hbm, hist_ref, local_sem.at[2])
    get_past.start()
    get_table = pltpu.make_async_copy(table_hbm, table, local_sem.at[0])
    get_mid = pltpu.make_async_copy(cmid_hbm, wraw, local_sem.at[1])
    get_table.start()
    get_mid.start()

    barrier = pltpu.get_barrier_semaphore()

    def greet(tm, strip):
        pl.semaphore_signal(
            barrier, inc=1, device_id=(tm, strip), device_id_type=pl.DeviceIdType.MESH
        )

    def greet_strips(k, _):
        greet(t, lax.rem(s + k, S))
        return 0

    lax.fori_loop(1, S, greet_strips, 0)

    for r in range(2):

        @pl.when(t != rows - 2 + r)
        def _():
            greet(rows - 2 + r, lax.rem(s + S - 1, S))

        @pl.when(t != r)
        def _():
            greet(r, lax.rem(s + 1, S))

    def greet_column(k, _):
        greet(lax.rem(t + k, T), s)
        return 0

    lax.fori_loop(1, T, greet_column, 0)

    for j in range(steps):
        for h in range(rows):
            xin[0, 2 + h, j] = traj_ref[pl.ds(j * CIN * rows + h, CIN, stride=rows), :].astype(BF16)
    send_down = to(xin.at[0, pl.ds(rows, 2)], xin.at[0, pl.ds(0, 2)], halo_send.at[0], halo_recv.at[0], t, s + 1)
    send_up = to(xin.at[0, pl.ds(2, 2)], xin.at[0, pl.ds(rows + 2, 2)], halo_send.at[1], halo_recv.at[1], t, s - 1)

    @pl.when(s == 0)
    def _():
        xin[0, 0:2] = jnp.zeros((2, steps, CIN, LANES), BF16)
        xin[1, 0:2] = jnp.zeros((2, steps, CIN, LANES), BF16)

    @pl.when(s == S - 1)
    def _():
        xin[0, rows + 2 : rows + 4] = jnp.zeros((2, steps, CIN, LANES), BF16)
        xin[1, rows + 2 : rows + 4] = jnp.zeros((2, steps, CIN, LANES), BF16)

    get_past.wait()

    for j in range(steps):
        length = jnp.full((CIN, LANES), hl_ref[j], jnp.int32)
        share = 1.0 / length.astype(F32)
        live = [jnp.where(length > m, share, 0.0) for m in range(3)]
        for h in range(rows):
            own = traj_ref[pl.ds(j * CIN * rows + h, CIN, stride=rows), :]
            past = [
                hist_ref[pl.ds((m * steps + j) * CIN * rows + h, CIN, stride=rows), :] for m in range(3)
            ]
            msend[h, j, 0:CIN] = own + (live[0] * past[0] + live[1] * past[1] + live[2] * past[2])
            msend[h, j, CIN : 2 * CIN] = live[1] * past[0] + live[2] * past[1] - live[0] * own
            msend[h, j, 2 * CIN : 2 * CIN + 8] = live[0][0:8]
    mrecv[t] = msend[t]

    row_id = lax.broadcasted_iota(jnp.int32, (CH, CH), 0)
    col_id = lax.broadcasted_iota(jnp.int32, (CH, CH), 1)
    diagonal = row_id == col_id
    gaincol[...] = jnp.sum(
        jnp.where(diagonal, jnp.broadcast_to(gain_ref[...].reshape(1, CH), (CH, CH)), 0.0), axis=1, keepdims=True
    )
    biascol[...] = jnp.sum(
        jnp.where(diagonal, jnp.broadcast_to(bias_ref[...].reshape(1, CH), (CH, CH)), 0.0), axis=1, keepdims=True
    )
    turned = lax.dot_general(
        diagonal.astype(F32).astype(BF16),
        cin_ref[...],
        (((1,), (1,)), ((), ())),
        preferred_element_type=F32,
    )
    win[...] = turned.astype(BF16)
    members = CH // GROUPS
    first = lax.broadcasted_iota(jnp.int32, (2 * CH, LANES), 1) * members
    channel = lax.broadcasted_iota(jnp.int32, (2 * CH, LANES), 0)
    ind[...] = jnp.where((channel >= first) & (channel < first + members), 1.0, 0.0)
    edge = (t < 2) | (t >= rows - 2)

    @pl.when(edge)
    def _():
        pl.semaphore_wait(barrier, S - 1 + 2 * (T - 1))

    @pl.when(jnp.logical_not(edge))
    def _():
        pl.semaphore_wait(barrier, S - 1 + T - 1)

    @pl.when(s < S - 1)
    def _():
        send_down.start()

    @pl.when(s > 0)
    def _():
        send_up.start()

    def send_m(k, _):
        other = lax.rem(t + k, T)
        to(msend.at[other], mrecv.at[t], m_send, m_recv, other, s).start()
        return 0

    lax.fori_loop(1, T, send_m, 0)

    get_table.wait()
    at = lax.broadcasted_iota(jnp.int32, table.shape, 1)
    for j in range(steps):
        embcol[j] = jnp.sum(jnp.where(at == ts_ref[j], table[...], 0.0), axis=1, keepdims=True)

    get_mid.wait()
    low = lax.broadcasted_iota(jnp.int32, (CH, LANES), 1) < 64
    for a in range(3):
        wmid[a, :, 0:256] = wraw[3 * a, :, 0:256]
        wmid[a, :, 640:960] = wraw[3 * a + 2]
        middle = [wraw[3 * a + 1, :, k * LANES : (k + 1) * LANES].astype(F32) for k in range(2)]
        tail = wraw[3 * a + 1, :, 256:320].astype(F32)
        middle.append(jnp.concatenate([tail, tail], axis=1))
        turned_by = [pltpu.roll(m, 64, 1) for m in middle[:2]] + [middle[2]]
        head = wraw[3 * a, :, 256:320].astype(F32)
        before = jnp.concatenate([head, head], axis=1)
        for k in range(3):
            wmid[a, :, 256 + k * LANES : 256 + (k + 1) * LANES] = jnp.where(
                low, before, turned_by[k]
            ).astype(BF16)
            before = turned_by[k]

    @pl.when(s < S - 1)
    def _():
        send_down.wait_send()

    @pl.when(s > 0)
    def _():
        send_up.wait_send()

    @pl.when(s > 0)
    def _():
        send_down.wait_recv()

    @pl.when(s < S - 1)
    def _():
        send_up.wait_recv()

    lane = lax.broadcasted_iota(jnp.int32, (CIN, LANES), 1)
    wide = lax.broadcasted_iota(jnp.int32, (CHUNK, LANES), 1)

    def shifted(x, lanes):
        zero = jnp.zeros_like(x)
        left = jnp.where(lanes == 0, zero, pltpu.roll(x, 1, 1))
        right = jnp.where(lanes == LANES - 1, zero, pltpu.roll(x, LANES - 1, 1))
        return left, right

    def first_conv(it, j):
        for r in range(rows + 4):
            block = xin[it, r, j]
            left, right = shifted(block.astype(F32), lane)
            xs[0:CIN, r * LANES : (r + 1) * LANES] = left.astype(BF16)
            xs[CIN : 2 * CIN, r * LANES : (r + 1) * LANES] = block
            xs[2 * CIN : 3 * CIN, r * LANES : (r + 1) * LANES] = right.astype(BF16)
        for r in range(0, rows + 2, 2):
            taps = jnp.concatenate(
                [xs[:, (r + a) * LANES : (r + a + 2) * LANES] for a in range(3)], axis=0
            )
            early[j, :, r * LANES : (r + 2) * LANES] = (
                jnp.dot(win[...], taps, preferred_element_type=F32) + embcol[j]
            )

    def send_sums(it, j):
        k = it * steps + j

        def add_up(c):
            at = c * CHUNK
            total = jnp.zeros((CHUNK, LANES), F32)
            square = jnp.zeros((CHUNK, LANES), F32)
            for r in range(1, rows + 1):
                x = early[j, pl.ds(at, CHUNK), r * LANES : (r + 1) * LANES]
                total += x
                square += x * x
            sums[pl.ds(at, CHUNK)] = total
            sums[pl.ds(CH + at, CHUNK)] = square

        for c in range(CH // CHUNK):
            add_up(c)
        ones = jnp.ones((8, LANES), BF16)
        by_channel = None
        for part in thirds(sums[...]):
            product = lax.dot_general(
                ones, part, (((1,), (1,)), ((), ())), preferred_element_type=F32
            )
            by_channel = product if by_channel is None else by_channel + product
        which = ind[...].astype(BF16)
        by_group = None
        for part in thirds(by_channel):
            product = jnp.dot(part, which, preferred_element_type=F32)
            by_group = product if by_group is None else by_group + product
        stat[k] = by_group[0:1]
        stats[k, s] = by_group[0:1]

        def send(i, _):
            other = lax.rem(s + i, S)
            to(stat.at[k], stats.at[k, s], s_send.at[k], s_recv.at[k], t, other).start()
            return 0

        lax.fori_loop(1, S, send, 0)

    def normalise(it, j):
        k = it * steps + j
        wait_bytes(stats.at[k, pl.ds(0, S - 1)], s_send.at[k])
        wait_bytes(stats.at[k, pl.ds(0, S - 1)], s_recv.at[k])
        total = jnp.sum(stats[k], axis=0) * (1.0 / count)
        total = jnp.broadcast_to(total, (8, LANES))
        variance = jnp.maximum(pltpu.roll(total, LANES - GROUPS, 1) - total * total, 0.0)
        scale = 1.0 / jnp.sqrt(variance + EPSILON)
        mean_row, scale_row = total[0:1], scale[0:1]

        def body(c):
            at = c * CHUNK
            which = ind[pl.ds(at, CHUNK)]
            mean = jnp.sum(jnp.where(which > 0.5, mean_row, 0.0), axis=1, keepdims=True)
            factor = jnp.sum(jnp.where(which > 0.5, scale_row, 0.0), axis=1, keepdims=True)
            factor = factor * gaincol[pl.ds(at, CHUNK)]
            offset = biascol[pl.ds(at, CHUNK)]
            for r in range(rows + 2):
                x = early[j, pl.ds(at, CHUNK), r * LANES : (r + 1) * LANES]
                x = silu((x - mean) * factor + offset)
                if r == 0:
                    x = jnp.where(s > 0, x, 0.0)
                if r == rows + 1:
                    x = jnp.where(s < S - 1, x, 0.0)
                x = x.astype(BF16)
                left, right = shifted(x, wide)
                cells = slice(r * LANES, (r + 1) * LANES)
                hid[j, pl.ds(at, CHUNK), cells] = left
                hid[j, pl.ds(CH + at, CHUNK), cells] = x
                hid[j, pl.ds(2 * CH + at, CHUNK), cells] = right

        for c in range(CH // CHUNK):
            body(c)

    def second_conv(it, j):
        late = None
        for a in range(3):
            product = jnp.dot(
                wmid[a], hid[j, :, a * LANES : (a + rows) * LANES], preferred_element_type=F32
            )
            late = product if late is None else late + product
        active = silu(late).astype(BF16)
        field = jnp.dot(cout_ref[...], active, preferred_element_type=F32)
        drift = field * step_ref[j]
        for h in range(rows):
            fsend[it, h, j] = drift[:, h * LANES : (h + 1) * LANES]

        def send(k, _):
            other = lax.rem(t + k, T)
            to(fsend.at[it, other, j], frecv.at[it, t, j], a_send.at[it], a_recv.at[it], other, s).start()
            return 0

        lax.fori_loop(1, T, send, 0)
        frecv[it, t, j] = fsend[it, t, j]

    def row_guess(it):
        wait_bytes(frecv.at[it, pl.ds(0, T - 1)], a_send.at[it])
        wait_bytes(frecv.at[it, pl.ds(0, T - 1)], a_recv.at[it])
        guess = [start_ref[pl.ds(t, CIN, stride=rows), :]]
        for i in range(total_steps - 1):
            guess.append(guess[-1] + frecv[it, i // steps, i % steps])
        return guess

    def mixed(guess, anchor, j):
        total = guess[j]
        for i in range(j + 1):
            total = total + (mix_ref[j, i].astype(F32) * UNIT) * anchor[i]
        return total

    for it in range(ITERS):
        for j in range(steps):
            first_conv(it, j)
            send_sums(it, j)
        for j in range(steps):
            normalise(it, j)
            second_conv(it, j)
        if it == 0:
            wait_bytes(mrecv.at[pl.ds(0, T - 1)], m_send)
            wait_bytes(mrecv.at[pl.ds(0, T - 1)], m_recv)
            guess = row_guess(it)
            anchor = [
                guess[i] - mrecv[i // steps, i % steps, 0:CIN] for i in range(total_steps)
            ]
            odd, after, before = lax.rem(t, 2), lax.rem(s + 1, S), lax.rem(s + S - 1, S)
            below = (t >= rows - 2) & (s < S - 1)
            above = (t < 2) & (s > 0)
            for k in range(T):
                for j in range(steps * k, steps * (k + 1)):
                    new = mixed(guess, anchor, j)
                    sbuf[j] = new.astype(BF16)
                    state1[j] = new
                pair = sbuf.at[pl.ds(steps * k, steps)]

                @pl.when(below)
                def _():
                    to(pair, xin.at[1, odd], b_send.at[1], b_recv.at[1], k, after).start()

                @pl.when(above)
                def _():
                    to(pair, xin.at[1, rows + 2 + odd], b_send.at[2], b_recv.at[2], k, before).start()

                @pl.when(t != k)
                def _():
                    to(pair, xin.at[1, 2 + t], b_send.at[0], b_recv.at[0], k, s).start()

            xin[1, 2 + t] = sbuf[pl.ds(steps * t, steps)]
            for j in range(total_steps):
                share = mrecv[j // steps, j % steps, 2 * CIN : 2 * CIN + 8]
                share = jnp.concatenate([share, share], axis=0)
                base2[j] = state1[j] + (share * guess[j] + mrecv[j // steps, j % steps, CIN : 2 * CIN])
            wait_bytes(sbuf.at[pl.ds(0, steps * (T - 1))], b_send.at[0])

            @pl.when(below)
            def _():
                wait_bytes(sbuf, b_send.at[1])

            @pl.when(above)
            def _():
                wait_bytes(sbuf, b_send.at[2])

            wait_bytes(sbuf.at[pl.ds(0, steps * (T - 1))], b_recv.at[0])

            @pl.when(s > 0)
            def _():
                wait_bytes(sbuf.at[pl.ds(0, steps * 2)], b_recv.at[1])

            @pl.when(s < S - 1)
            def _():
                wait_bytes(sbuf.at[pl.ds(0, steps * 2)], b_recv.at[2])

        else:
            guess = row_guess(it)
            anchor = [guess[i] - base2[i] for i in range(total_steps)]
            for k in range(T):
                for j in range(steps * k, steps * (k + 1)):
                    osend[j, 1] = guess[j] - state1[j]
                    osend[j, 0] = mixed(guess, anchor, j)

                @pl.when(t != k)
                def _():
                    to(osend.at[pl.ds(steps * k, steps)], orecv.at[t], o_send, o_recv, k, s).start()

            orecv[t] = osend[pl.ds(steps * t, steps)]
            wait_bytes(orecv.at[pl.ds(0, T - 1)], o_send)
            wait_bytes(orecv.at[pl.ds(0, T - 1)], o_recv)
            for j in range(steps):
                for h in range(rows):
                    iterate_ref[pl.ds(j * CIN * rows + h, CIN, stride=rows), :] = orecv[h, j, 0]
                    residual_ref[pl.ds(j * CIN * rows + h, CIN, stride=rows), :] = orecv[h, j, 1]


def solution(mesh):
    T = mesh.shape["tm"]
    S = mesh.shape["strip"]

    def shards(
        start_state,
        trajectory,
        history,
        history_length,
        timesteps,
        step_size,
        mix_table,
        time_table,
        conv_in,
        norm_gain,
        norm_bias,
        conv_mid,
        conv_out,
    ):
        steps, CIN, rows, width = trajectory.shape
        CH = conv_out.shape[1]
        total = steps * T
        flat = steps * CIN * rows
        smem = pl.BlockSpec(memory_space=pltpu.SMEM)
        vmem = pl.BlockSpec(memory_space=pltpu.VMEM)
        hbm = pl.BlockSpec(memory_space=pl.ANY)
        dma = pltpu.SemaphoreType.DMA
        iterate, residual = pl.pallas_call(
            functools.partial(kernel, T, S),
            out_shape=(pltpu.VMEM((flat, width), F32),) * 2,
            in_specs=[smem] * 4 + [vmem] * 6 + [hbm] * 3,
            out_specs=(vmem, vmem),
            scratch_shapes=[
                pltpu.VMEM((history.shape[0] * flat, width), F32),
                pltpu.VMEM((CH, time_table.shape[0]), F32),
                pltpu.VMEM((9, CH, CH), BF16),
                pltpu.VMEM((3, CH, 3 * CH), BF16),
                pltpu.VMEM((CH, 9 * CIN), BF16),
                pltpu.VMEM((ITERS, rows + 4, steps, CIN, width), BF16),
                pltpu.VMEM((3 * CIN, (rows + 4) * width), BF16),
                pltpu.VMEM((steps, CH, (rows + 2) * width), F32),
                pltpu.VMEM((steps, 3 * CH, (rows + 2) * width), BF16),
                pltpu.VMEM((CH, 1), F32),
                pltpu.VMEM((CH, 1), F32),
                pltpu.VMEM((steps, CH, 1), F32),
                pltpu.VMEM((2 * CH, width), F32),
                pltpu.VMEM((2 * CH, width), F32),
                pltpu.VMEM((ITERS * steps, 1, width), F32),
                pltpu.VMEM((ITERS * steps, S, 1, width), F32),
                pltpu.VMEM((ITERS, rows, steps, CIN, width), F32),
                pltpu.VMEM((ITERS, T, steps, CIN, width), F32),
                pltpu.VMEM((rows, steps, 2 * CIN + 8, width), F32),
                pltpu.VMEM((T, steps, 2 * CIN + 8, width), F32),
                pltpu.VMEM((total, CIN, width), BF16),
                pltpu.VMEM((total, CIN, width), F32),
                pltpu.VMEM((total, CIN, width), F32),
                pltpu.VMEM((total, 2, CIN, width), F32),
                pltpu.VMEM((rows, steps, 2, CIN, width), F32),
                dma((3,)),
                dma((2,)),
                dma((2,)),
                dma,
                dma,
                dma((ITERS * steps,)),
                dma((ITERS * steps,)),
                dma((ITERS,)),
                dma((ITERS,)),
                dma((3,)),
                dma((3,)),
                dma,
                dma,
            ],
            compiler_params=pltpu.CompilerParams(
                collective_id=0, has_side_effects=True, vmem_limit_bytes=56 * 1024 * 1024
            ),
        )(
            history_length,
            timesteps,
            step_size,
            mix_table,
            norm_gain,
            norm_bias,
            start_state.reshape(CIN * rows, width),
            trajectory.reshape(flat, width),
            jnp.swapaxes(conv_in, 1, 2).reshape(9 * CIN, CH),
            conv_out,
            time_table.T,
            conv_mid,
            history.reshape(history.shape[0] * flat, width),
        )
        valid = history_length[0] > 0
        return (
            jnp.where(valid, iterate, residual).reshape(trajectory.shape),
            jnp.where(valid, residual, iterate).reshape(trajectory.shape),
        )

    return jax.shard_map(
        shards,
        mesh=mesh,
        in_specs=(
            P(None, "strip", None),
            P("tm", None, "strip", None),
            P(None, "tm", None, "strip", None),
            P("tm"),
            P("tm"),
            P("tm"),
            P(),
            P(),
            P(),
            P(),
            P(),
            P(),
            P(),
        ),
        out_specs=(P("tm", None, "strip", None), P("tm", None, "strip", None)),
        check_vma=False,
    )
```

```python
import functools

import jax
import jax.numpy as jnp
from jax import lax
from jax.experimental import pallas as pl
from jax.experimental.pallas import tpu as pltpu
from jax.sharding import PartitionSpec as P

F32 = jnp.float32
BF16 = jnp.bfloat16
GROUPS = 32
ITERS = 2
EPSILON = 1e-05
UNIT = 1.0 / 256.0
LANES = 128
CHUNK = 32


def silu(v):
    half = 0.5 * v
    return half + half * jnp.tanh(half)


def thirds(x):
    high = x.astype(BF16)
    rest = x - high.astype(F32)
    middle = rest.astype(BF16)
    return high, middle, (rest - middle.astype(F32)).astype(BF16)


def kernel(
    T,
    S,
    hl_ref,
    ts_ref,
    step_ref,
    mix_ref,
    gain_ref,
    bias_ref,
    start_ref,
    traj_ref,
    cin_ref,
    cout_ref,
    table_hbm,
    cmid_hbm,
    hist_hbm,
    iterate_ref,
    residual_ref,
    hist_ref,
    table,
    wraw,
    wmid,
    win,
    xin,
    xs,
    early,
    hid,
    gaincol,
    biascol,
    embcol,
    ind,
    sums,
    stat,
    stats,
    fsend,
    frecv,
    msend,
    mrecv,
    sbuf,
    state1,
    base2,
    osend,
    orecv,
    local_sem,
    halo_send,
    halo_recv,
    m_send,
    m_recv,
    s_send,
    s_recv,
    a_send,
    a_recv,
    b_send,
    b_recv,
    o_send,
    o_recv,
):
    t = lax.axis_index("tm")
    s = lax.axis_index("strip")
    steps = 2
    CH = cout_ref.shape[1]
    CIN = cout_ref.shape[0]
    rows = T
    total_steps = steps * T
    count = float(CH // GROUPS * rows * S * LANES)

    def to(src, dst, send, recv, tm, strip):
        return pltpu.make_async_remote_copy(
            src_ref=src,
            dst_ref=dst,
            send_sem=send,
            recv_sem=recv,
            device_id=(tm, strip),
            device_id_type=pl.DeviceIdType.MESH,
        )

    def wait_bytes(ref, sem):
        pltpu.make_async_copy(ref, ref, sem).wait()

    get_past = pltpu.make_async_copy(hist_hbm, hist_ref, local_sem.at[2])
    get_past.start()
    get_table = pltpu.make_async_copy(table_hbm, table, local_sem.at[0])
    get_mid = pltpu.make_async_copy(cmid_hbm, wraw, local_sem.at[1])
    get_table.start()
    get_mid.start()

    barrier = pltpu.get_barrier_semaphore()

    def greet(tm, strip):
        pl.semaphore_signal(
            barrier, inc=1, device_id=(tm, strip), device_id_type=pl.DeviceIdType.MESH
        )

    def greet_strips(k, _):
        greet(t, lax.rem(s + k, S))
        return 0

    lax.fori_loop(1, S, greet_strips, 0)

    for r in range(2):

        @pl.when(t != rows - 2 + r)
        def _():
            greet(rows - 2 + r, lax.rem(s + S - 1, S))

        @pl.when(t != r)
        def _():
            greet(r, lax.rem(s + 1, S))

    def greet_column(k, _):
        greet(lax.rem(t + k, T), s)
        return 0

    lax.fori_loop(1, T, greet_column, 0)

    for j in range(steps):
        for h in range(rows):
            xin[0, 2 + h, j] = traj_ref[pl.ds(j * CIN * rows + h, CIN, stride=rows), :].astype(BF16)
    send_down = to(xin.at[0, pl.ds(rows, 2)], xin.at[0, pl.ds(0, 2)], halo_send.at[0], halo_recv.at[0], t, s + 1)
    send_up = to(xin.at[0, pl.ds(2, 2)], xin.at[0, pl.ds(rows + 2, 2)], halo_send.at[1], halo_recv.at[1], t, s - 1)

    @pl.when(s == 0)
    def _():
        xin[0, 0:2] = jnp.zeros((2, steps, CIN, LANES), BF16)
        xin[1, 0:2] = jnp.zeros((2, steps, CIN, LANES), BF16)

    @pl.when(s == S - 1)
    def _():
        xin[0, rows + 2 : rows + 4] = jnp.zeros((2, steps, CIN, LANES), BF16)
        xin[1, rows + 2 : rows + 4] = jnp.zeros((2, steps, CIN, LANES), BF16)

    get_past.wait()

    for j in range(steps):
        length = jnp.full((CIN, LANES), hl_ref[j], jnp.int32)
        share = 1.0 / length.astype(F32)
        live = [jnp.where(length > m, share, 0.0) for m in range(3)]
        for h in range(rows):
            own = traj_ref[pl.ds(j * CIN * rows + h, CIN, stride=rows), :]
            past = [
                hist_ref[pl.ds((m * steps + j) * CIN * rows + h, CIN, stride=rows), :] for m in range(3)
            ]
            msend[h, j, 0:CIN] = own + (live[0] * past[0] + live[1] * past[1] + live[2] * past[2])
            msend[h, j, CIN : 2 * CIN] = live[1] * past[0] + live[2] * past[1] - live[0] * own
            msend[h, j, 2 * CIN : 2 * CIN + 8] = live[0][0:8]
    mrecv[t] = msend[t]

    row_id = lax.broadcasted_iota(jnp.int32, (CH, CH), 0)
    col_id = lax.broadcasted_iota(jnp.int32, (CH, CH), 1)
    diagonal = row_id == col_id
    gaincol[...] = jnp.sum(
        jnp.where(diagonal, jnp.broadcast_to(gain_ref[...].reshape(1, CH), (CH, CH)), 0.0), axis=1, keepdims=True
    )
    biascol[...] = jnp.sum(
        jnp.where(diagonal, jnp.broadcast_to(bias_ref[...].reshape(1, CH), (CH, CH)), 0.0), axis=1, keepdims=True
    )
    turned = lax.dot_general(
        diagonal.astype(F32).astype(BF16),
        cin_ref[...],
        (((1,), (1,)), ((), ())),
        preferred_element_type=F32,
    )
    win[...] = turned.astype(BF16)
    members = CH // GROUPS
    first = lax.broadcasted_iota(jnp.int32, (2 * CH, LANES), 1) * members
    channel = lax.broadcasted_iota(jnp.int32, (2 * CH, LANES), 0)
    ind[...] = jnp.where((channel >= first) & (channel < first + members), 1.0, 0.0)
    edge = (t < 2) | (t >= rows - 2)

    @pl.when(edge)
    def _():
        pl.semaphore_wait(barrier, S - 1 + 2 * (T - 1))

    @pl.when(jnp.logical_not(edge))
    def _():
        pl.semaphore_wait(barrier, S - 1 + T - 1)

    @pl.when(s < S - 1)
    def _():
        send_down.start()

    @pl.when(s > 0)
    def _():
        send_up.start()

    def send_m(k, _):
        other = lax.rem(t + k, T)
        to(msend.at[other], mrecv.at[t], m_send, m_recv, other, s).start()
        return 0

    lax.fori_loop(1, T, send_m, 0)

    get_table.wait()
    at = lax.broadcasted_iota(jnp.int32, table.shape, 1)
    for j in range(steps):
        embcol[j] = jnp.sum(jnp.where(at == ts_ref[j], table[...], 0.0), axis=1, keepdims=True)

    get_mid.wait()
    low = lax.broadcasted_iota(jnp.int32, (CH, LANES), 1) < 64
    for a in range(3):
        wmid[a, :, 0:256] = wraw[3 * a, :, 0:256]
        wmid[a, :, 640:960] = wraw[3 * a + 2]
        middle = [wraw[3 * a + 1, :, k * LANES : (k + 1) * LANES].astype(F32) for k in range(2)]
        tail = wraw[3 * a + 1, :, 256:320].astype(F32)
        middle.append(jnp.concatenate([tail, tail], axis=1))
        turned_by = [pltpu.roll(m, 64, 1) for m in middle[:2]] + [middle[2]]
        head = wraw[3 * a, :, 256:320].astype(F32)
        before = jnp.concatenate([head, head], axis=1)
        for k in range(3):
            wmid[a, :, 256 + k * LANES : 256 + (k + 1) * LANES] = jnp.where(
                low, before, turned_by[k]
            ).astype(BF16)
            before = turned_by[k]

    lane = lax.broadcasted_iota(jnp.int32, (CIN, LANES), 1)
    wide = lax.broadcasted_iota(jnp.int32, (CHUNK, LANES), 1)

    def shifted(x, lanes):
        zero = jnp.zeros_like(x)
        left = jnp.where(lanes == 0, zero, pltpu.roll(x, 1, 1))
        right = jnp.where(lanes == LANES - 1, zero, pltpu.roll(x, LANES - 1, 1))
        return left, right

    def first_conv(it, j, rows_in, rows_out):
        for r in rows_in:
            block = xin[it, r, j]
            left, right = shifted(block.astype(F32), lane)
            xs[j, 0:CIN, r * LANES : (r + 1) * LANES] = left.astype(BF16)
            xs[j, CIN : 2 * CIN, r * LANES : (r + 1) * LANES] = block
            xs[j, 2 * CIN : 3 * CIN, r * LANES : (r + 1) * LANES] = right.astype(BF16)
        for r in rows_out:
            taps = jnp.concatenate(
                [xs[j, :, (r + a) * LANES : (r + a + 2) * LANES] for a in range(3)], axis=0
            )
            early[j, :, r * LANES : (r + 2) * LANES] = (
                jnp.dot(win[...], taps, preferred_element_type=F32) + embcol[j]
            )

    def inner_rows(it):
        for j in range(steps):
            first_conv(it, j, range(2, rows + 2), range(2, rows, 2))

    def outer_rows(it, j):
        first_conv(it, j, (0, 1, rows + 2, rows + 3), (0, rows))

    inner_rows(0)

    @pl.when(s < S - 1)
    def _():
        send_down.wait_send()

    @pl.when(s > 0)
    def _():
        send_up.wait_send()

    @pl.when(s > 0)
    def _():
        send_down.wait_recv()

    @pl.when(s < S - 1)
    def _():
        send_up.wait_recv()

    def send_sums(it, j):
        k = it * steps + j

        def add_up(c):
            at = c * CHUNK
            total = jnp.zeros((CHUNK, LANES), F32)
            square = jnp.zeros((CHUNK, LANES), F32)
            for r in range(1, rows + 1):
                x = early[j, pl.ds(at, CHUNK), r * LANES : (r + 1) * LANES]
                total += x
                square += x * x
            sums[pl.ds(at, CHUNK)] = total
            sums[pl.ds(CH + at, CHUNK)] = square

        for c in range(CH // CHUNK):
            add_up(c)
        ones = jnp.ones((8, LANES), BF16)
        by_channel = None
        for part in thirds(sums[...]):
            product = lax.dot_general(
                ones, part, (((1,), (1,)), ((), ())), preferred_element_type=F32
            )
            by_channel = product if by_channel is None else by_channel + product
        which = ind[...].astype(BF16)
        by_group = None
        for part in thirds(by_channel):
            product = jnp.dot(part, which, preferred_element_type=F32)
            by_group = product if by_group is None else by_group + product
        stat[k] = by_group[0:1]
        stats[k, s] = by_group[0:1]

        def send(i, _):
            other = lax.rem(s + i, S)
            to(stat.at[k], stats.at[k, s], s_send.at[k], s_recv.at[k], t, other).start()
            return 0

        lax.fori_loop(1, S, send, 0)

    def normalise(it, j):
        k = it * steps + j
        wait_bytes(stats.at[k, pl.ds(0, S - 1)], s_send.at[k])
        wait_bytes(stats.at[k, pl.ds(0, S - 1)], s_recv.at[k])
        total = jnp.sum(stats[k], axis=0) * (1.0 / count)
        total = jnp.broadcast_to(total, (8, LANES))
        variance = jnp.maximum(pltpu.roll(total, LANES - GROUPS, 1) - total * total, 0.0)
        scale = 1.0 / jnp.sqrt(variance + EPSILON)
        mean_row, scale_row = total[0:1], scale[0:1]

        def body(c):
            at = c * CHUNK
            which = ind[pl.ds(at, CHUNK)]
            mean = jnp.sum(jnp.where(which > 0.5, mean_row, 0.0), axis=1, keepdims=True)
            factor = jnp.sum(jnp.where(which > 0.5, scale_row, 0.0), axis=1, keepdims=True)
            factor = factor * gaincol[pl.ds(at, CHUNK)]
            offset = biascol[pl.ds(at, CHUNK)]
            for r in range(rows + 2):
                x = early[j, pl.ds(at, CHUNK), r * LANES : (r + 1) * LANES]
                x = silu((x - mean) * factor + offset)
                if r == 0:
                    x = jnp.where(s > 0, x, 0.0)
                if r == rows + 1:
                    x = jnp.where(s < S - 1, x, 0.0)
                x = x.astype(BF16)
                left, right = shifted(x, wide)
                cells = slice(r * LANES, (r + 1) * LANES)
                hid[j, pl.ds(at, CHUNK), cells] = left
                hid[j, pl.ds(CH + at, CHUNK), cells] = x
                hid[j, pl.ds(2 * CH + at, CHUNK), cells] = right

        for c in range(CH // CHUNK):
            body(c)

    def second_conv(it, j):
        late = None
        for a in range(3):
            product = jnp.dot(
                wmid[a], hid[j, :, a * LANES : (a + rows) * LANES], preferred_element_type=F32
            )
            late = product if late is None else late + product
        active = silu(late).astype(BF16)
        field = jnp.dot(cout_ref[...], active, preferred_element_type=F32)
        drift = field * step_ref[j]
        for h in range(rows):
            fsend[it, h, j] = drift[:, h * LANES : (h + 1) * LANES]

        def send(k, _):
            other = lax.rem(t + k, T)
            to(fsend.at[it, other, j], frecv.at[it, t, j], a_send.at[it], a_recv.at[it], other, s).start()
            return 0

        lax.fori_loop(1, T, send, 0)
        frecv[it, t, j] = fsend[it, t, j]

    def row_guess(it):
        wait_bytes(frecv.at[it, pl.ds(0, T - 1)], a_send.at[it])
        wait_bytes(frecv.at[it, pl.ds(0, T - 1)], a_recv.at[it])
        guess = [start_ref[pl.ds(t, CIN, stride=rows), :]]
        for i in range(total_steps - 1):
            guess.append(guess[-1] + frecv[it, i // steps, i % steps])
        return guess

    def mixed(guess, anchor, j):
        total = guess[j]
        for i in range(j + 1):
            total = total + (mix_ref[j, i].astype(F32) * UNIT) * anchor[i]
        return total

    for it in range(ITERS):
        for j in range(steps):
            outer_rows(it, j)
            send_sums(it, j)
        for j in range(steps):
            normalise(it, j)
            second_conv(it, j)
        if it == 0:
            wait_bytes(mrecv.at[pl.ds(0, T - 1)], m_send)
            wait_bytes(mrecv.at[pl.ds(0, T - 1)], m_recv)
            guess = row_guess(it)
            anchor = [
                guess[i] - mrecv[i // steps, i % steps, 0:CIN] for i in range(total_steps)
            ]
            odd, after, before = lax.rem(t, 2), lax.rem(s + 1, S), lax.rem(s + S - 1, S)
            below = (t >= rows - 2) & (s < S - 1)
            above = (t < 2) & (s > 0)
            for k in range(T):
                for j in range(steps * k, steps * (k + 1)):
                    new = mixed(guess, anchor, j)
                    sbuf[j] = new.astype(BF16)
                    state1[j] = new
                pair = sbuf.at[pl.ds(steps * k, steps)]

                @pl.when(below)
                def _():
                    to(pair, xin.at[1, odd], b_send.at[1], b_recv.at[1], k, after).start()

                @pl.when(above)
                def _():
                    to(pair, xin.at[1, rows + 2 + odd], b_send.at[2], b_recv.at[2], k, before).start()

                @pl.when(t != k)
                def _():
                    to(pair, xin.at[1, 2 + t], b_send.at[0], b_recv.at[0], k, s).start()

            xin[1, 2 + t] = sbuf[pl.ds(steps * t, steps)]
            for j in range(total_steps):
                share = mrecv[j // steps, j % steps, 2 * CIN : 2 * CIN + 8]
                share = jnp.concatenate([share, share], axis=0)
                base2[j] = state1[j] + (share * guess[j] + mrecv[j // steps, j % steps, CIN : 2 * CIN])
            wait_bytes(sbuf.at[pl.ds(0, steps * (T - 1))], b_send.at[0])

            @pl.when(below)
            def _():
                wait_bytes(sbuf, b_send.at[1])

            @pl.when(above)
            def _():
                wait_bytes(sbuf, b_send.at[2])

            wait_bytes(sbuf.at[pl.ds(0, steps * (T - 1))], b_recv.at[0])
            inner_rows(1)

            @pl.when(s > 0)
            def _():
                wait_bytes(sbuf.at[pl.ds(0, steps * 2)], b_recv.at[1])

            @pl.when(s < S - 1)
            def _():
                wait_bytes(sbuf.at[pl.ds(0, steps * 2)], b_recv.at[2])

        else:
            guess = row_guess(it)
            anchor = [guess[i] - base2[i] for i in range(total_steps)]
            for k in range(T):
                for j in range(steps * k, steps * (k + 1)):
                    osend[j, 1] = guess[j] - state1[j]
                    osend[j, 0] = mixed(guess, anchor, j)

                @pl.when(t != k)
                def _():
                    to(osend.at[pl.ds(steps * k, steps)], orecv.at[t], o_send, o_recv, k, s).start()

            orecv[t] = osend[pl.ds(steps * t, steps)]
            wait_bytes(orecv.at[pl.ds(0, T - 1)], o_send)
            wait_bytes(orecv.at[pl.ds(0, T - 1)], o_recv)
            for j in range(steps):
                for h in range(rows):
                    iterate_ref[pl.ds(j * CIN * rows + h, CIN, stride=rows), :] = orecv[h, j, 0]
                    residual_ref[pl.ds(j * CIN * rows + h, CIN, stride=rows), :] = orecv[h, j, 1]


def solution(mesh):
    T = mesh.shape["tm"]
    S = mesh.shape["strip"]

    def shards(
        start_state,
        trajectory,
        history,
        history_length,
        timesteps,
        step_size,
        mix_table,
        time_table,
        conv_in,
        norm_gain,
        norm_bias,
        conv_mid,
        conv_out,
    ):
        steps, CIN, rows, width = trajectory.shape
        CH = conv_out.shape[1]
        total = steps * T
        flat = steps * CIN * rows
        smem = pl.BlockSpec(memory_space=pltpu.SMEM)
        vmem = pl.BlockSpec(memory_space=pltpu.VMEM)
        hbm = pl.BlockSpec(memory_space=pl.ANY)
        dma = pltpu.SemaphoreType.DMA
        iterate, residual = pl.pallas_call(
            functools.partial(kernel, T, S),
            out_shape=(pltpu.VMEM((flat, width), F32),) * 2,
            in_specs=[smem] * 4 + [vmem] * 6 + [hbm] * 3,
            out_specs=(vmem, vmem),
            scratch_shapes=[
                pltpu.VMEM((history.shape[0] * flat, width), F32),
                pltpu.VMEM((CH, time_table.shape[0]), F32),
                pltpu.VMEM((9, CH, CH), BF16),
                pltpu.VMEM((3, CH, 3 * CH), BF16),
                pltpu.VMEM((CH, 9 * CIN), BF16),
                pltpu.VMEM((ITERS, rows + 4, steps, CIN, width), BF16),
                pltpu.VMEM((steps, 3 * CIN, (rows + 4) * width), BF16),
                pltpu.VMEM((steps, CH, (rows + 2) * width), F32),
                pltpu.VMEM((steps, 3 * CH, (rows + 2) * width), BF16),
                pltpu.VMEM((CH, 1), F32),
                pltpu.VMEM((CH, 1), F32),
                pltpu.VMEM((steps, CH, 1), F32),
                pltpu.VMEM((2 * CH, width), F32),
                pltpu.VMEM((2 * CH, width), F32),
                pltpu.VMEM((ITERS * steps, 1, width), F32),
                pltpu.VMEM((ITERS * steps, S, 1, width), F32),
                pltpu.VMEM((ITERS, rows, steps, CIN, width), F32),
                pltpu.VMEM((ITERS, T, steps, CIN, width), F32),
                pltpu.VMEM((rows, steps, 2 * CIN + 8, width), F32),
                pltpu.VMEM((T, steps, 2 * CIN + 8, width), F32),
                pltpu.VMEM((total, CIN, width), BF16),
                pltpu.VMEM((total, CIN, width), F32),
                pltpu.VMEM((total, CIN, width), F32),
                pltpu.VMEM((total, 2, CIN, width), F32),
                pltpu.VMEM((rows, steps, 2, CIN, width), F32),
                dma((3,)),
                dma((2,)),
                dma((2,)),
                dma,
                dma,
                dma((ITERS * steps,)),
                dma((ITERS * steps,)),
                dma((ITERS,)),
                dma((ITERS,)),
                dma((3,)),
                dma((3,)),
                dma,
                dma,
            ],
            compiler_params=pltpu.CompilerParams(
                collective_id=0, has_side_effects=True, vmem_limit_bytes=56 * 1024 * 1024
            ),
        )(
            history_length,
            timesteps,
            step_size,
            mix_table,
            norm_gain,
            norm_bias,
            start_state.reshape(CIN * rows, width),
            trajectory.reshape(flat, width),
            jnp.swapaxes(conv_in, 1, 2).reshape(9 * CIN, CH),
            conv_out,
            time_table.T,
            conv_mid,
            history.reshape(history.shape[0] * flat, width),
        )
        valid = history_length[0] > 0
        return (
            jnp.where(valid, iterate, residual).reshape(trajectory.shape),
            jnp.where(valid, residual, iterate).reshape(trajectory.shape),
        )

    return jax.shard_map(
        shards,
        mesh=mesh,
        in_specs=(
            P(None, "strip", None),
            P("tm", None, "strip", None),
            P(None, "tm", None, "strip", None),
            P("tm"),
            P("tm"),
            P("tm"),
            P(),
            P(),
            P(),
            P(),
            P(),
            P(),
            P(),
        ),
        out_specs=(P("tm", None, "strip", None), P("tm", None, "strip", None)),
        check_vma=False,
    )
```

```python
import functools

import jax
import jax.numpy as jnp
from jax import lax
from jax.experimental import pallas as pl
from jax.experimental.pallas import tpu as pltpu
from jax.sharding import PartitionSpec as P

F32 = jnp.float32
BF16 = jnp.bfloat16
GROUPS = 32
ITERS = 2
EPSILON = 1e-05
UNIT = 1.0 / 256.0
LANES = 128
CHUNK = 32


def silu(v):
    half = 0.5 * v
    return half + half * jnp.tanh(half)


def thirds(x):
    high = x.astype(BF16)
    rest = x - high.astype(F32)
    middle = rest.astype(BF16)
    return high, middle, (rest - middle.astype(F32)).astype(BF16)


def kernel(
    T,
    S,
    hl_ref,
    ts_ref,
    step_ref,
    mix_ref,
    gain_ref,
    bias_ref,
    start_ref,
    traj_ref,
    cin_ref,
    cout_ref,
    table_hbm,
    cmid_hbm,
    hist_hbm,
    iterate_ref,
    residual_ref,
    hist_ref,
    table,
    wraw,
    wmid,
    win,
    xin,
    xs,
    early,
    hid,
    gaincol,
    biascol,
    embcol,
    ind,
    sums,
    stat,
    stats,
    fsend,
    frecv,
    msend,
    mrecv,
    sbuf,
    state1,
    base2,
    osend,
    orecv,
    local_sem,
    halo_send,
    halo_recv,
    m_send,
    m_recv,
    s_send,
    s_recv,
    a_send,
    a_recv,
    b_send,
    b_recv,
    o_send,
    o_recv,
):
    t = lax.axis_index("tm")
    s = lax.axis_index("strip")
    steps = 2
    CH = cout_ref.shape[1]
    CIN = cout_ref.shape[0]
    rows = T
    total_steps = steps * T
    count = float(CH // GROUPS * rows * S * LANES)

    def to(src, dst, send, recv, tm, strip):
        return pltpu.make_async_remote_copy(
            src_ref=src,
            dst_ref=dst,
            send_sem=send,
            recv_sem=recv,
            device_id=(tm, strip),
            device_id_type=pl.DeviceIdType.MESH,
        )

    def wait_bytes(ref, sem):
        pltpu.make_async_copy(ref, ref, sem).wait()

    get_past = pltpu.make_async_copy(hist_hbm, hist_ref, local_sem.at[2])
    get_past.start()
    get_table = pltpu.make_async_copy(table_hbm, table, local_sem.at[0])
    get_mid = pltpu.make_async_copy(cmid_hbm, wraw, local_sem.at[1])
    get_table.start()
    get_mid.start()

    barrier = pltpu.get_barrier_semaphore()

    def greet(tm, strip):
        pl.semaphore_signal(
            barrier, inc=1, device_id=(tm, strip), device_id_type=pl.DeviceIdType.MESH
        )

    def greet_strips(k, _):
        greet(t, lax.rem(s + k, S))
        return 0

    lax.fori_loop(1, S, greet_strips, 0)

    for r in range(2):

        @pl.when(t != rows - 2 + r)
        def _():
            greet(rows - 2 + r, lax.rem(s + S - 1, S))

        @pl.when(t != r)
        def _():
            greet(r, lax.rem(s + 1, S))

    def greet_column(k, _):
        greet(lax.rem(t + k, T), s)
        return 0

    lax.fori_loop(1, T, greet_column, 0)

    for j in range(steps):
        for h in range(rows):
            xin[0, 2 + h, j] = traj_ref[pl.ds(j * CIN * rows + h, CIN, stride=rows), :].astype(BF16)
    send_down = to(xin.at[0, pl.ds(rows, 2)], xin.at[0, pl.ds(0, 2)], halo_send.at[0], halo_recv.at[0], t, s + 1)
    send_up = to(xin.at[0, pl.ds(2, 2)], xin.at[0, pl.ds(rows + 2, 2)], halo_send.at[1], halo_recv.at[1], t, s - 1)

    @pl.when(s == 0)
    def _():
        xin[0, 0:2] = jnp.zeros((2, steps, CIN, LANES), BF16)
        xin[1, 0:2] = jnp.zeros((2, steps, CIN, LANES), BF16)

    @pl.when(s == S - 1)
    def _():
        xin[0, rows + 2 : rows + 4] = jnp.zeros((2, steps, CIN, LANES), BF16)
        xin[1, rows + 2 : rows + 4] = jnp.zeros((2, steps, CIN, LANES), BF16)

    get_past.wait()

    for j in range(steps):
        length = jnp.full((CIN, LANES), hl_ref[j], jnp.int32)
        share = 1.0 / length.astype(F32)
        live = [jnp.where(length > m, share, 0.0) for m in range(3)]
        for h in range(rows):
            own = traj_ref[pl.ds(j * CIN * rows + h, CIN, stride=rows), :]
            past = [
                hist_ref[pl.ds((m * steps + j) * CIN * rows + h, CIN, stride=rows), :] for m in range(3)
            ]
            msend[h, j, 0:CIN] = own + (live[0] * past[0] + live[1] * past[1] + live[2] * past[2])
            msend[h, j, CIN : 2 * CIN] = live[1] * past[0] + live[2] * past[1] - live[0] * own
            msend[h, j, 2 * CIN : 2 * CIN + 8] = live[0][0:8]
    mrecv[t] = msend[t]

    row_id = lax.broadcasted_iota(jnp.int32, (CH, CH), 0)
    col_id = lax.broadcasted_iota(jnp.int32, (CH, CH), 1)
    diagonal = row_id == col_id
    gaincol[...] = jnp.sum(
        jnp.where(diagonal, jnp.broadcast_to(gain_ref[...].reshape(1, CH), (CH, CH)), 0.0), axis=1, keepdims=True
    )
    biascol[...] = jnp.sum(
        jnp.where(diagonal, jnp.broadcast_to(bias_ref[...].reshape(1, CH), (CH, CH)), 0.0), axis=1, keepdims=True
    )
    turned = lax.dot_general(
        diagonal.astype(F32).astype(BF16),
        cin_ref[...],
        (((1,), (1,)), ((), ())),
        preferred_element_type=F32,
    )
    win[...] = turned.astype(BF16)
    members = CH // GROUPS
    first = lax.broadcasted_iota(jnp.int32, (2 * CH, LANES), 1) * members
    channel = lax.broadcasted_iota(jnp.int32, (2 * CH, LANES), 0)
    ind[...] = jnp.where((channel >= first) & (channel < first + members), 1.0, 0.0)
    edge = (t < 2) | (t >= rows - 2)

    @pl.when(edge)
    def _():
        pl.semaphore_wait(barrier, S - 1 + 2 * (T - 1))

    @pl.when(jnp.logical_not(edge))
    def _():
        pl.semaphore_wait(barrier, S - 1 + T - 1)

    @pl.when(s < S - 1)
    def _():
        send_down.start()

    @pl.when(s > 0)
    def _():
        send_up.start()

    def send_m(k, _):
        other = lax.rem(t + k, T)
        to(msend.at[other], mrecv.at[t], m_send, m_recv, other, s).start()
        return 0

    lax.fori_loop(1, T, send_m, 0)

    get_table.wait()
    at = lax.broadcasted_iota(jnp.int32, table.shape, 1)
    for j in range(steps):
        embcol[j] = jnp.sum(jnp.where(at == ts_ref[j], table[...], 0.0), axis=1, keepdims=True)

    get_mid.wait()
    low = lax.broadcasted_iota(jnp.int32, (CH, LANES), 1) < 64
    for a in range(3):
        wmid[a, :, 0:256] = wraw[3 * a, :, 0:256]
        wmid[a, :, 640:960] = wraw[3 * a + 2]
        middle = [wraw[3 * a + 1, :, k * LANES : (k + 1) * LANES].astype(F32) for k in range(2)]
        tail = wraw[3 * a + 1, :, 256:320].astype(F32)
        middle.append(jnp.concatenate([tail, tail], axis=1))
        turned_by = [pltpu.roll(m, 64, 1) for m in middle[:2]] + [middle[2]]
        head = wraw[3 * a, :, 256:320].astype(F32)
        before = jnp.concatenate([head, head], axis=1)
        for k in range(3):
            wmid[a, :, 256 + k * LANES : 256 + (k + 1) * LANES] = jnp.where(
                low, before, turned_by[k]
            ).astype(BF16)
            before = turned_by[k]

    lane = lax.broadcasted_iota(jnp.int32, (CIN, LANES), 1)
    wide = lax.broadcasted_iota(jnp.int32, (CHUNK, LANES), 1)

    def shifted(x, lanes):
        zero = jnp.zeros_like(x)
        left = jnp.where(lanes == 0, zero, pltpu.roll(x, 1, 1))
        right = jnp.where(lanes == LANES - 1, zero, pltpu.roll(x, LANES - 1, 1))
        return left, right

    def first_conv(it, j, rows_in, rows_out):
        for r in rows_in:
            block = xin[it, r, j]
            left, right = shifted(block.astype(F32), lane)
            xs[j, 0:CIN, r * LANES : (r + 1) * LANES] = left.astype(BF16)
            xs[j, CIN : 2 * CIN, r * LANES : (r + 1) * LANES] = block
            xs[j, 2 * CIN : 3 * CIN, r * LANES : (r + 1) * LANES] = right.astype(BF16)
        for r in rows_out:
            taps = jnp.concatenate(
                [xs[j, :, (r + a) * LANES : (r + a + 2) * LANES] for a in range(3)], axis=0
            )
            early[j, :, r * LANES : (r + 2) * LANES] = (
                jnp.dot(win[...], taps, preferred_element_type=F32) + embcol[j]
            )

    def add_up(j, rows_in, fresh):
        for at in range(0, CH, CHUNK):
            total = square = jnp.zeros((CHUNK, LANES), F32)
            if not fresh:
                total, square = sums[j, pl.ds(at, CHUNK)], sums[j, pl.ds(CH + at, CHUNK)]
            for r in rows_in:
                x = early[j, pl.ds(at, CHUNK), r * LANES : (r + 1) * LANES]
                total += x
                square += x * x
            sums[j, pl.ds(at, CHUNK)] = total
            sums[j, pl.ds(CH + at, CHUNK)] = square

    def inner_rows(it):
        for j in range(steps):
            first_conv(it, j, range(2, rows + 2), range(2, rows, 2))
            add_up(j, range(2, rows), True)

    def outer_rows(it, j):
        first_conv(it, j, (0, 1, rows + 2, rows + 3), (0, rows))

    inner_rows(0)

    @pl.when(s < S - 1)
    def _():
        send_down.wait_send()

    @pl.when(s > 0)
    def _():
        send_up.wait_send()

    @pl.when(s > 0)
    def _():
        send_down.wait_recv()

    @pl.when(s < S - 1)
    def _():
        send_up.wait_recv()

    def send_sums(it, j):
        k = it * steps + j

        add_up(j, (1, rows), False)
        ones = jnp.ones((8, LANES), BF16)
        by_channel = None
        for part in thirds(sums[j]):
            product = lax.dot_general(
                ones, part, (((1,), (1,)), ((), ())), preferred_element_type=F32
            )
            by_channel = product if by_channel is None else by_channel + product
        which = ind[...].astype(BF16)
        by_group = None
        for part in thirds(by_channel):
            product = jnp.dot(part, which, preferred_element_type=F32)
            by_group = product if by_group is None else by_group + product
        stat[k] = by_group[0:1]
        stats[k, s] = by_group[0:1]

        def send(i, _):
            other = lax.rem(s + i, S)
            to(stat.at[k], stats.at[k, s], s_send.at[k], s_recv.at[k], t, other).start()
            return 0

        lax.fori_loop(1, S, send, 0)

    def normalise(it, j):
        k = it * steps + j
        wait_bytes(stats.at[k, pl.ds(0, S - 1)], s_send.at[k])
        wait_bytes(stats.at[k, pl.ds(0, S - 1)], s_recv.at[k])
        total = jnp.sum(stats[k], axis=0) * (1.0 / count)
        total = jnp.broadcast_to(total, (8, LANES))
        variance = jnp.maximum(pltpu.roll(total, LANES - GROUPS, 1) - total * total, 0.0)
        scale = 1.0 / jnp.sqrt(variance + EPSILON)
        mean_row, scale_row = total[0:1], scale[0:1]

        def body(c):
            at = c * CHUNK
            which = ind[pl.ds(at, CHUNK)]
            mean = jnp.sum(jnp.where(which > 0.5, mean_row, 0.0), axis=1, keepdims=True)
            factor = jnp.sum(jnp.where(which > 0.5, scale_row, 0.0), axis=1, keepdims=True)
            factor = factor * gaincol[pl.ds(at, CHUNK)]
            offset = biascol[pl.ds(at, CHUNK)]
            for r in range(rows + 2):
                x = early[j, pl.ds(at, CHUNK), r * LANES : (r + 1) * LANES]
                x = silu((x - mean) * factor + offset)
                if r == 0:
                    x = jnp.where(s > 0, x, 0.0)
                if r == rows + 1:
                    x = jnp.where(s < S - 1, x, 0.0)
                x = x.astype(BF16)
                left, right = shifted(x, wide)
                cells = slice(r * LANES, (r + 1) * LANES)
                hid[j, pl.ds(at, CHUNK), cells] = left
                hid[j, pl.ds(CH + at, CHUNK), cells] = x
                hid[j, pl.ds(2 * CH + at, CHUNK), cells] = right

        for c in range(CH // CHUNK):
            body(c)

    def second_conv(it, j):
        late = None
        for a in range(3):
            product = jnp.dot(
                wmid[a], hid[j, :, a * LANES : (a + rows) * LANES], preferred_element_type=F32
            )
            late = product if late is None else late + product
        active = silu(late).astype(BF16)
        field = jnp.dot(cout_ref[...], active, preferred_element_type=F32)
        drift = field * step_ref[j]
        for h in range(rows):
            fsend[it, h, j] = drift[:, h * LANES : (h + 1) * LANES]

        def send(k, _):
            other = lax.rem(t + k, T)
            to(fsend.at[it, other, j], frecv.at[it, t, j], a_send.at[it], a_recv.at[it], other, s).start()
            return 0

        lax.fori_loop(1, T, send, 0)
        frecv[it, t, j] = fsend[it, t, j]

    def row_guess(it):
        wait_bytes(frecv.at[it, pl.ds(0, T - 1)], a_send.at[it])
        wait_bytes(frecv.at[it, pl.ds(0, T - 1)], a_recv.at[it])
        guess = [start_ref[pl.ds(t, CIN, stride=rows), :]]
        for i in range(total_steps - 1):
            guess.append(guess[-1] + frecv[it, i // steps, i % steps])
        return guess

    def mixed(guess, anchor, j):
        total = guess[j]
        for i in range(j + 1):
            total = total + (mix_ref[j, i].astype(F32) * UNIT) * anchor[i]
        return total

    for it in range(ITERS):
        for j in range(steps):
            outer_rows(it, j)
            send_sums(it, j)
        for j in range(steps):
            normalise(it, j)
            second_conv(it, j)
        if it == 0:
            wait_bytes(mrecv.at[pl.ds(0, T - 1)], m_send)
            wait_bytes(mrecv.at[pl.ds(0, T - 1)], m_recv)
            guess = row_guess(it)
            anchor = [
                guess[i] - mrecv[i // steps, i % steps, 0:CIN] for i in range(total_steps)
            ]
            odd, after, before = lax.rem(t, 2), lax.rem(s + 1, S), lax.rem(s + S - 1, S)
            below = (t >= rows - 2) & (s < S - 1)
            above = (t < 2) & (s > 0)
            for k in range(T):
                for j in range(steps * k, steps * (k + 1)):
                    new = mixed(guess, anchor, j)
                    sbuf[j] = new.astype(BF16)
                    state1[j] = new
                pair = sbuf.at[pl.ds(steps * k, steps)]

                @pl.when(below)
                def _():
                    to(pair, xin.at[1, odd], b_send.at[1], b_recv.at[1], k, after).start()

                @pl.when(above)
                def _():
                    to(pair, xin.at[1, rows + 2 + odd], b_send.at[2], b_recv.at[2], k, before).start()

                @pl.when(t != k)
                def _():
                    to(pair, xin.at[1, 2 + t], b_send.at[0], b_recv.at[0], k, s).start()

            xin[1, 2 + t] = sbuf[pl.ds(steps * t, steps)]
            for j in range(total_steps):
                share = mrecv[j // steps, j % steps, 2 * CIN : 2 * CIN + 8]
                share = jnp.concatenate([share, share], axis=0)
                base2[j] = state1[j] + (share * guess[j] + mrecv[j // steps, j % steps, CIN : 2 * CIN])
            wait_bytes(sbuf.at[pl.ds(0, steps * (T - 1))], b_send.at[0])

            @pl.when(below)
            def _():
                wait_bytes(sbuf, b_send.at[1])

            @pl.when(above)
            def _():
                wait_bytes(sbuf, b_send.at[2])

            wait_bytes(sbuf.at[pl.ds(0, steps * (T - 1))], b_recv.at[0])
            inner_rows(1)

            @pl.when(s > 0)
            def _():
                wait_bytes(sbuf.at[pl.ds(0, steps * 2)], b_recv.at[1])

            @pl.when(s < S - 1)
            def _():
                wait_bytes(sbuf.at[pl.ds(0, steps * 2)], b_recv.at[2])

        else:
            guess = row_guess(it)
            anchor = [guess[i] - base2[i] for i in range(total_steps)]
            for k in range(T):
                for j in range(steps * k, steps * (k + 1)):
                    osend[j, 1] = guess[j] - state1[j]
                    osend[j, 0] = mixed(guess, anchor, j)

                @pl.when(t != k)
                def _():
                    to(osend.at[pl.ds(steps * k, steps)], orecv.at[t], o_send, o_recv, k, s).start()

            orecv[t] = osend[pl.ds(steps * t, steps)]
            wait_bytes(orecv.at[pl.ds(0, T - 1)], o_send)
            wait_bytes(orecv.at[pl.ds(0, T - 1)], o_recv)
            for j in range(steps):
                for h in range(rows):
                    iterate_ref[pl.ds(j * CIN * rows + h, CIN, stride=rows), :] = orecv[h, j, 0]
                    residual_ref[pl.ds(j * CIN * rows + h, CIN, stride=rows), :] = orecv[h, j, 1]


def solution(mesh):
    T = mesh.shape["tm"]
    S = mesh.shape["strip"]

    def shards(
        start_state,
        trajectory,
        history,
        history_length,
        timesteps,
        step_size,
        mix_table,
        time_table,
        conv_in,
        norm_gain,
        norm_bias,
        conv_mid,
        conv_out,
    ):
        steps, CIN, rows, width = trajectory.shape
        CH = conv_out.shape[1]
        total = steps * T
        flat = steps * CIN * rows
        smem = pl.BlockSpec(memory_space=pltpu.SMEM)
        vmem = pl.BlockSpec(memory_space=pltpu.VMEM)
        hbm = pl.BlockSpec(memory_space=pl.ANY)
        dma = pltpu.SemaphoreType.DMA
        iterate, residual = pl.pallas_call(
            functools.partial(kernel, T, S),
            out_shape=(pltpu.VMEM((flat, width), F32),) * 2,
            in_specs=[smem] * 4 + [vmem] * 6 + [hbm] * 3,
            out_specs=(vmem, vmem),
            scratch_shapes=[
                pltpu.VMEM((history.shape[0] * flat, width), F32),
                pltpu.VMEM((CH, time_table.shape[0]), F32),
                pltpu.VMEM((9, CH, CH), BF16),
                pltpu.VMEM((3, CH, 3 * CH), BF16),
                pltpu.VMEM((CH, 9 * CIN), BF16),
                pltpu.VMEM((ITERS, rows + 4, steps, CIN, width), BF16),
                pltpu.VMEM((steps, 3 * CIN, (rows + 4) * width), BF16),
                pltpu.VMEM((steps, CH, (rows + 2) * width), F32),
                pltpu.VMEM((steps, 3 * CH, (rows + 2) * width), BF16),
                pltpu.VMEM((CH, 1), F32),
                pltpu.VMEM((CH, 1), F32),
                pltpu.VMEM((steps, CH, 1), F32),
                pltpu.VMEM((2 * CH, width), F32),
                pltpu.VMEM((steps, 2 * CH, width), F32),
                pltpu.VMEM((ITERS * steps, 1, width), F32),
                pltpu.VMEM((ITERS * steps, S, 1, width), F32),
                pltpu.VMEM((ITERS, rows, steps, CIN, width), F32),
                pltpu.VMEM((ITERS, T, steps, CIN, width), F32),
                pltpu.VMEM((rows, steps, 2 * CIN + 8, width), F32),
                pltpu.VMEM((T, steps, 2 * CIN + 8, width), F32),
                pltpu.VMEM((total, CIN, width), BF16),
                pltpu.VMEM((total, CIN, width), F32),
                pltpu.VMEM((total, CIN, width), F32),
                pltpu.VMEM((total, 2, CIN, width), F32),
                pltpu.VMEM((rows, steps, 2, CIN, width), F32),
                dma((3,)),
                dma((2,)),
                dma((2,)),
                dma,
                dma,
                dma((ITERS * steps,)),
                dma((ITERS * steps,)),
                dma((ITERS,)),
                dma((ITERS,)),
                dma((3,)),
                dma((3,)),
                dma,
                dma,
            ],
            compiler_params=pltpu.CompilerParams(
                collective_id=0, has_side_effects=True, vmem_limit_bytes=56 * 1024 * 1024
            ),
        )(
            history_length,
            timesteps,
            step_size,
            mix_table,
            norm_gain,
            norm_bias,
            start_state.reshape(CIN * rows, width),
            trajectory.reshape(flat, width),
            jnp.swapaxes(conv_in, 1, 2).reshape(9 * CIN, CH),
            conv_out,
            time_table.T,
            conv_mid,
            history.reshape(history.shape[0] * flat, width),
        )
        valid = history_length[0] > 0
        return (
            jnp.where(valid, iterate, residual).reshape(trajectory.shape),
            jnp.where(valid, residual, iterate).reshape(trajectory.shape),
        )

    return jax.shard_map(
        shards,
        mesh=mesh,
        in_specs=(
            P(None, "strip", None),
            P("tm", None, "strip", None),
            P(None, "tm", None, "strip", None),
            P("tm"),
            P("tm"),
            P("tm"),
            P(),
            P(),
            P(),
            P(),
            P(),
            P(),
            P(),
        ),
        out_specs=(P("tm", None, "strip", None), P("tm", None, "strip", None)),
        check_vma=False,
    )
```
